128 devices in a mesh: group: 8 (over y, core), tile: 16 (over x, z).
Axes of the slice: x: 4, y: 4, z: 4, core: 2. Of those that a mesh axis runs over, the one named last changes fastest.
Arguments:
- embeddings: bfloat16 [49152, 768], P(('group', 'tile')), may hold values from -15 to 15
- clusters: int32 [49152], P(('group', 'tile')), may hold values from 0 to 31, as said below
- cluster_owner: int32 [32], replicated, may hold values from 0 to 7, as said below
Outputs:
- neighbours: bfloat16 [49152, 768], P(('group', 'tile'))
- log_mass: float32 [49152], P(('group', 'tile'))
The draws below stay inside these ranges and needn't reach their ends.
Inputs may be any that keep to these rules, and one draw needn't show every extreme that they name: Among the 384 rows of one device at most 72 belong to clusters of any one group; in every draw one group has exactly 72 rows on every device. `cluster_owner`: each group owns exactly 4 clusters.
All inputs are finite; a program needn't handle non-finite values.
Results may differ from the reference program's by a relative error of at most 0.034.
Values may be sent and summed in bfloat16 or wider, within the bound.
No kernel may reach another device: no remote copies, remote signals or barrier semaphores. Data moves between devices by JAX's collectives and lax.ppermute only.
A program may use at most 128 MiB of HBM per device.

```python
import math
import jax
import jax.numpy as jnp
from jax import lax

D = 768
ROW_DEV = 384
CPG = 4
GROUPS = 8
CAP = 72
SLOTS = 576
ROWS = 49152
CLUSTERS = 32


def layout(base_key):
    perm_key, pref_key, full_key, score_key, rows_key, pick_key = jax.random.split(base_key, 6)
    labels = jax.random.permutation(perm_key, CLUSTERS).astype(jnp.int32)
    owners = labels % GROUPS
    members = jnp.argsort(labels, stable=True).astype(jnp.int32)
    prefer = jax.random.randint(pref_key, (GROUPS,), 1, 4)
    fullest = jax.random.randint(full_key, (), 0, GROUPS)
    blocks = ROWS // ROW_DEV
    slot_group = jnp.arange(SLOTS, dtype=jnp.int32) // CAP
    draw_noise = jax.random.randint(score_key, (blocks, SLOTS), 0, 16384)
    ranked = draw_noise * jnp.take(prefer, slot_group)[None, :]
    ranked = jnp.where(slot_group[None, :] == fullest, -1, ranked)
    ranked = ranked * SLOTS + jnp.arange(SLOTS, dtype=jnp.int32)[None, :]
    chosen = jnp.argsort(ranked, axis=1, stable=True)[:, :ROW_DEV].astype(jnp.int32)
    mixing = jax.random.randint(rows_key, (blocks, ROW_DEV), 0, 1048576) * ROW_DEV + jnp.arange(ROW_DEV, dtype=jnp.int32)[None, :]
    order_rows = jnp.argsort(mixing, axis=1, stable=True)
    slot_ids = jnp.take_along_axis(chosen, order_rows, axis=1)
    dest_group = slot_ids // CAP
    pick_index = jax.random.randint(pick_key, (blocks, ROW_DEV), 0, CPG)
    row_clusters = jnp.take(members, dest_group + GROUPS * pick_index)
    return (row_clusters.reshape(ROWS).astype(jnp.int32), owners.astype(jnp.int32))


def draw_clusters(key, part):
    return layout(jax.random.fold_in(key, 7))[0]


def draw_cluster_owner(key, part):
    return layout(jax.random.fold_in(key, 7))[1]


def draw_embeddings(key, part):
    drawn_rows = jax.random.normal(jax.random.fold_in(key, 11), (ROWS, D), jnp.float32)
    return jnp.clip(drawn_rows, -6.0, 6.0).astype(jnp.bfloat16)


def setup_inputs(seed: int = 0) -> dict:
    arg_keys = jax.random.split(jax.random.key(seed), 4)
    embeddings = draw_embeddings(jax.random.fold_in(arg_keys[3], 71), 0)
    clusters = draw_clusters(jax.random.fold_in(arg_keys[3], 71), 0)
    cluster_owner = draw_cluster_owner(jax.random.fold_in(arg_keys[3], 71), 0)
    return {"embeddings": embeddings, "clusters": clusters, "cluster_owner": cluster_owner}


score_scale = 3.0
penalty = 2.0

def block_results(query_rows, query_ids, query_pos, key_rows, key_ids, key_pos):
    products = jnp.dot(query_rows, key_rows.T, preferred_element_type=jnp.float32)
    differs = (query_ids[:, None] != key_ids[None, :]).astype(jnp.float32)
    scores = products * (score_scale / math.sqrt(D)) - penalty * differs
    usable = (key_ids[None, :] >= 0) & (key_pos[None, :] != query_pos[:, None])
    row_peak = lax.optimization_barrier(jnp.max(jnp.where(usable, scores, 0.0), axis=1))
    weights = jnp.exp(jnp.where(usable, scores - row_peak[:, None], -jnp.inf))
    row_total = jnp.exp(-row_peak) + lax.optimization_barrier(jnp.sum(weights, axis=1))
    log_values = row_peak + jnp.log(row_total)
    weighted = jnp.dot(weights.astype(jnp.bfloat16), key_rows, preferred_element_type=jnp.float32)
    return ((weighted / row_total[:, None]).astype(jnp.bfloat16), log_values)

def reference(embeddings, clusters, cluster_owner):
    blocks = ROWS // ROW_DEV
    group_of = jnp.take(cluster_owner, clusters).astype(jnp.int32)
    dest_group = group_of.reshape(blocks, ROW_DEV)
    same_group = dest_group[:, :, None] == dest_group[:, None, :]
    row_index = jnp.arange(ROW_DEV, dtype=jnp.int32)
    earlier = row_index[None, :] < row_index[:, None]
    rank_in = lax.optimization_barrier(jnp.sum(same_group & earlier[None, :, :], axis=2)).astype(jnp.int32)
    source = jnp.broadcast_to(jnp.arange(blocks, dtype=jnp.int32)[:, None], (blocks, ROW_DEV)).reshape(-1)
    flat_dest = dest_group.reshape(-1)
    flat_rank = rank_in.reshape(-1)
    all_rows = jnp.arange(ROWS, dtype=jnp.int32)
    holder = jnp.full((GROUPS, blocks, CAP), -1, dtype=jnp.int32).at[flat_dest, source, flat_rank].set(all_rows)
    group_slots = holder.reshape(GROUPS, blocks * CAP)

    def one_group(key_pos):
        safe_index = jnp.maximum(key_pos, 0)
        key_rows = jnp.take(embeddings, safe_index, axis=0)
        key_ids = jnp.where(key_pos >= 0, jnp.take(clusters, safe_index), -1).astype(jnp.int32)

        def per_block(block_number):
            first_slot = block_number * SLOTS
            query_rows = lax.dynamic_slice_in_dim(key_rows, first_slot, SLOTS, 0)
            query_ids = lax.dynamic_slice_in_dim(key_ids, first_slot, SLOTS, 0)
            query_pos = lax.dynamic_slice_in_dim(key_pos, first_slot, SLOTS, 0)
            return block_results(query_rows, query_ids, query_pos, key_rows, key_ids, key_pos)
        return lax.map(per_block, jnp.arange(blocks * CAP // SLOTS, dtype=jnp.int32))
    mixed, log_values = lax.map(one_group, group_slots)
    flat_mixed = mixed.reshape(GROUPS * blocks * CAP, D)
    flat_log = log_values.reshape(-1)
    where_row = flat_dest * (blocks * CAP) + source * CAP + flat_rank
    return (jnp.take(flat_mixed, where_row, axis=0), jnp.take(flat_log, where_row))
```

```python
import functools
import math

import jax
import jax.numpy as jnp
from jax import lax
from jax.experimental import pallas as pl
from jax.experimental.pallas import tpu as pltpu
from jax.sharding import PartitionSpec as P

score_scale = 3.0
penalty = 2.0
log2e = math.log2(math.e)
ln2 = math.log(2.0)
masked = -1e30
axes = ("group", "tile")
part_rows = 24
parts = 3
packet_rows = 80
block_keys = 192
block_rows = 208
f32 = jnp.float32
bf16 = jnp.bfloat16


def vmem_specs(count):
    return [pl.BlockSpec(memory_space=pltpu.VMEM) for _ in range(count)]


params = pltpu.CompilerParams(vmem_limit_bytes=48 * 1024 * 1024)


def row_facts(clusters_ref, owner_ref, me):
    cluster = clusters_ref[...]
    rows = cluster.shape[1]
    group = jnp.zeros_like(cluster)
    for number in range(owner_ref.shape[0]):
        group = jnp.where(cluster == number, owner_ref[number], group)
    member = lax.broadcasted_iota(jnp.int32, (8, rows), 0) == group
    upper = lax.broadcasted_iota(jnp.int32, (rows, rows), 0) < lax.broadcasted_iota(
        jnp.int32, (rows, rows), 1
    )
    counts = jnp.dot(
        member.astype(f32).astype(bf16), upper.astype(f32).astype(bf16), preferred_element_type=f32
    )
    rank = jnp.sum(jnp.where(member, counts, 0.0), axis=0, keepdims=True).astype(jnp.int32)
    part = (rank >= part_rows).astype(jnp.int32) + (rank >= 2 * part_rows).astype(jnp.int32)
    lane = me * part_rows + rank - part * part_rows
    return cluster, group, rank, part, lane


def hits(count, target):
    shape = (count, target.shape[1])
    return lax.broadcasted_iota(jnp.int32, shape, 0) == target


def ones_at(count, target):
    return hits(count, target).astype(f32).astype(bf16)


def place_kernel(me_ref, owner_ref, clusters_ref, rows_ref, out_ref):
    cluster, group, rank, part, lane = row_facts(clusters_ref, owner_ref, me_ref[0])
    width = rows_ref.shape[1]
    total = out_ref.shape[0]
    placed = jnp.dot(
        ones_at(total, group * packet_rows + rank), rows_ref[...], preferred_element_type=f32
    )
    labels = jnp.where(hits(64, group * 8 + part), (cluster + 1).astype(f32), 0.0).astype(bf16)
    ids = lax.dot_general(
        labels, ones_at(width, lane), (((1,), (1,)), ((), ())), preferred_element_type=f32
    ).astype(bf16)
    source = lax.broadcasted_iota(jnp.int32, (1, 64), 1)
    placed_ids = jnp.dot(
        ones_at(total, (source // 8) * packet_rows + 72 + source % 8), ids, preferred_element_type=f32
    )
    out_ref[...] = (placed + placed_ids).astype(bf16)


def pack_kernel(in_ref, q_ref, *part_refs):
    packets = [in_ref[s].astype(f32) for s in range(8)]
    for p in range(parts):
        rows = [packets[s][p * part_rows : (p + 1) * part_rows] for s in range(8)]
        ids = packets[0][72:80]
        for s in range(1, 8):
            ids = ids + packets[s][72:80]
        at = lax.broadcasted_iota(jnp.int32, ids.shape, 0)
        row = jnp.sum(jnp.where(at == p, ids, 0.0), axis=0, keepdims=True)
        tail = jnp.where(at == 0, row, 0.0)
        block = jnp.concatenate(rows + [tail, jnp.zeros_like(tail)], axis=0).astype(bf16)
        part_refs[p][...] = block
        q_ref[p * block_rows : (p + 1) * block_rows, :] = block


def column_of(row):
    count = block_keys
    wide = row.shape[1]
    eye = lax.broadcasted_iota(jnp.int32, (count, wide), 0) == lax.broadcasted_iota(
        jnp.int32, (count, wide), 1
    )
    return jnp.sum(jnp.where(eye, row, 0.0), axis=1, keepdims=True)


def row_of(column, wide):
    count = column.shape[0]
    eye = lax.broadcasted_iota(jnp.int32, (count, wide), 0) == lax.broadcasted_iota(
        jnp.int32, (count, wide), 1
    )
    return jnp.sum(jnp.where(eye, column, 0.0), axis=0, keepdims=True)


def high_low(value):
    high = value.astype(bf16).astype(f32)
    return high, value - high


def flash_kernel(blocks, chunk, first, own, finish, *refs):
    refs = list(refs)
    q_ref = refs.pop(0)
    key_refs = [refs.pop(0) for _ in blocks]
    if not first:
        m_in, l_in, acc_in = refs.pop(0), refs.pop(0), refs.pop(0)
    if finish:
        out_ref = refs.pop(0)
    else:
        m_out, l_out, acc_out = refs.pop(0), refs.pop(0), refs.pop(0)
    keys = refs.pop(0)
    width = q_ref.shape[1]
    scale = score_scale / math.sqrt(width) * log2e
    id_rows = []
    number = 0
    for ref, count in zip(key_refs, blocks):
        for b in range(count):
            keys[number * block_keys : (number + 1) * block_keys, :] = ref[
                b * block_rows : b * block_rows + block_keys, :
            ]
            ids = ref[b * block_rows + block_keys : (b + 1) * block_rows, 0:256].astype(f32)
            id_rows.append(ids[0:8])
            number += 1
    pieces = []
    for b in range(0, number, 2):
        even = id_rows[b]
        odd = pltpu.roll(id_rows[b + 1], 64, 1)
        pieces += [even[:, 0:128], even[:, 128:256] + odd[:, 0:128], odd[:, 128:256]]
    key_id = jnp.concatenate(pieces, axis=1)[0:1]
    other = jnp.where(key_id == 0.0, masked, -penalty * log2e)
    total_keys = number * block_keys
    for p in range(parts):
        q = q_ref[p * block_rows : p * block_rows + block_keys, :]
        q_ids = q_ref[p * block_rows + block_keys : (p + 1) * block_rows, 0:256].astype(f32)
        q_id = column_of(q_ids[0:1])
        at = slice(p * block_keys, (p + 1) * block_keys)
        if first:
            peak = jnp.zeros((block_keys, 1), f32)
            mass = jnp.full((block_keys, 1), 1.0 if own else 0.0, f32)
            acc = None
        else:
            peak, mass, acc = m_in[at, :], l_in[at, :], acc_in[at, :]
        for start in range(0, total_keys, chunk):
            span = slice(start, start + chunk)
            scores = lax.dot_general(
                q, keys[span, :], (((1,), (1,)), ((), ())), preferred_element_type=f32
            )
            scores = scores * scale + jnp.where(key_id[:, span] == q_id, 0.0, other[:, span])
            if first and own and start <= p * block_keys < start + chunk:
                row = lax.broadcasted_iota(jnp.int32, scores.shape, 0) + (p * block_keys - start)
                scores = jnp.where(row == lax.broadcasted_iota(jnp.int32, scores.shape, 1), masked, scores)
            new_peak = jnp.maximum(peak, jnp.max(scores, axis=1, keepdims=True))
            weights = jnp.exp2(scores - new_peak)
            fade = jnp.exp2(peak - new_peak)
            mass = mass * fade + jnp.sum(weights, axis=1, keepdims=True)
            mixed = jnp.dot(weights.astype(bf16), keys[span, :], preferred_element_type=f32)
            acc = mixed if acc is None else acc * fade + mixed
            peak = new_peak
        if finish:
            safe = jnp.where(mass > 0.0, mass, 1.0)
            out_ref[at, :] = (acc / safe).astype(bf16)
            level = jnp.where(mass > 0.0, peak + jnp.log2(safe), masked)
            high, low = high_low(level)
            pair = [row_of(high, width), row_of(low, width)]
            here = lax.broadcasted_iota(jnp.int32, (16, width), 0)
            tail = jnp.where(here == 2 * p, pair[0], 0.0) + jnp.where(here == 2 * p + 1, pair[1], 0.0)
            tails = tail if p == 0 else tails + tail
        else:
            m_out[at, :], l_out[at, :], acc_out[at, :] = peak, mass, acc
    if finish:
        rows = parts * block_keys
        out_ref[rows : rows + 16, :] = tails.astype(bf16)


def flash(q, key_arrays, state, own, finish):
    width = q.shape[1]
    blocks = [a.shape[0] // block_rows for a in key_arrays]
    total = sum(blocks) * block_keys
    rows = parts * block_keys
    first = state is None
    if finish:
        outs = [jax.ShapeDtypeStruct((rows + 16, width), bf16)]
    else:
        outs = [
            jax.ShapeDtypeStruct((rows, 1), f32),
            jax.ShapeDtypeStruct((rows, 1), f32),
            jax.ShapeDtypeStruct((rows, width), f32),
        ]
    args = [q, *key_arrays] + ([] if first else list(state))
    out = pl.pallas_call(
        functools.partial(flash_kernel, blocks, 1152, first, own, finish),
        out_shape=outs,
        in_specs=vmem_specs(len(args)),
        out_specs=vmem_specs(len(outs)),
        scratch_shapes=[pltpu.VMEM((total, width), bf16)],
        compiler_params=params,
        cost_estimate=pl.CostEstimate(
            flops=4 * rows * total * width,
            transcendentals=rows * total,
            bytes_accessed=2 * total * width + 6 * rows * width,
        ),
        name="flash",
    )(*args)
    return out[0] if finish else tuple(out)


def combine_kernel(m_ref, l_ref, acc_ref, other_ref, out_ref):
    width = acc_ref.shape[1]
    rows = parts * block_keys
    tails = other_ref[rows : rows + 16, :].astype(f32)
    mixes, levels = [], []
    here = lax.broadcasted_iota(jnp.int32, (8, width), 0)
    for p in range(parts):
        at = slice(p * block_keys, (p + 1) * block_keys)
        level = column_of(
            tails[2 * p : 2 * p + 1, 0:256] + tails[2 * p + 1 : 2 * p + 2, 0:256]
        )
        peak = jnp.maximum(m_ref[at, :], level)
        mine = jnp.exp2(m_ref[at, :] - peak)
        theirs = jnp.exp2(level - peak)
        total = l_ref[at, :] * mine + theirs
        mixes.append(
            (acc_ref[at, :] * mine + other_ref[at, :].astype(f32) * theirs) / total
        )
        high, low = high_low((peak + jnp.log2(total)) * ln2)
        tail = jnp.where(here == p, row_of(high, width), 0.0) + jnp.where(
            here == 3 + p, row_of(low, width), 0.0
        )
        levels = tail if p == 0 else levels + tail
    for s in range(8):
        pieces = [m[s * part_rows : (s + 1) * part_rows] for m in mixes] + [levels]
        out_ref[s] = jnp.concatenate(pieces, axis=0).astype(bf16)


def final_kernel(me_ref, owner_ref, clusters_ref, back_ref, rows_ref, mass_ref):
    _, group, rank, part, lane = row_facts(clusters_ref, owner_ref, me_ref[0])
    total = back_ref.shape[0]
    rows_ref[...] = lax.dot_general(
        ones_at(total, group * packet_rows + rank),
        back_ref[...],
        (((0,), (0,)), ((), ())),
        preferred_element_type=f32,
    ).astype(bf16)
    levels = jnp.concatenate(
        [
            back_ref[g * packet_rows + 64 : (g + 1) * packet_rows, 0:256].astype(f32)[8:16]
            for g in range(8)
        ],
        axis=0,
    ).astype(bf16)
    found = jnp.dot(levels, ones_at(256, lane), preferred_element_type=f32)
    chosen = hits(64, group * 8 + part) | hits(64, group * 8 + 3 + part)
    mass_ref[...] = jnp.sum(jnp.where(chosen, found, 0.0), axis=0, keepdims=True)


def links(mesh):
    side = 4

    def number(y, c, x, z):
        return ((y * 2 + c) * side + x) * side + z

    places = [
        (y, c, x, z) for y in range(side) for c in range(2) for x in range(side) for z in range(side)
    ]

    def pairs(move):
        return [(number(*at), number(*move(*at))) for at in places]

    dims = [
        pairs(lambda y, c, x, z: (y, c, x ^ 3, z)),
        pairs(lambda y, c, x, z: (y, c, x, z ^ 1)),
        pairs(lambda y, c, x, z: (y, c, x, z ^ 3)),
    ]
    swap = pairs(lambda y, c, x, z: (y, c ^ 1, x, z))
    groups = []
    for c in range(2):
        for half in range(2):
            for z in range(side):
                groups.append(
                    [
                        number(y, c, 2 * half + (kind ^ half), z)
                        for y in range(side)
                        for kind in range(2)
                    ]
                )
    return dims, swap, groups


def per_device(dims, swap, groups, embeddings, clusters, cluster_owner):
    rows, width = embeddings.shape
    send = lambda a, pairs: lax.ppermute(a, axes, pairs)
    group_axis, tile = lax.axis_index("group"), lax.axis_index("tile")
    x = tile // 4
    kind = ((x + 1) // 2) % 2
    me = ((group_axis // 2) * 2 + kind).astype(jnp.int32).reshape(1)
    cluster_row = clusters.reshape(1, rows)
    smem = pl.BlockSpec(memory_space=pltpu.SMEM)
    packets = pl.pallas_call(
        place_kernel,
        out_shape=jax.ShapeDtypeStruct((8 * packet_rows, width), bf16),
        in_specs=[smem, smem] + vmem_specs(2),
        out_specs=vmem_specs(1)[0],
        compiler_params=params,
        name="place",
    )(me, cluster_owner, cluster_row, embeddings)
    arrived = lax.all_to_all(
        packets.reshape(8, packet_rows, width), axes, 0, 0, axis_index_groups=groups, tiled=True
    )
    q_own, *pieces = pl.pallas_call(
        pack_kernel,
        out_shape=[jax.ShapeDtypeStruct((parts * block_rows, width), bf16)]
        + [jax.ShapeDtypeStruct((block_rows, width), bf16)] * parts,
        in_specs=vmem_specs(1),
        out_specs=vmem_specs(1 + parts),
        compiler_params=params,
        name="pack",
    )(arrived)
    near = [send(pieces[p], dims[p]) for p in range(parts)]
    q_other = send(q_own, swap)
    two = [jnp.concatenate([pieces[p], near[p]], axis=0) for p in range(parts)]
    second = [send(two[p], dims[(p + 1) % 3]) for p in range(parts)]
    third = [send(two[p], dims[(p + 2) % 3]) for p in range(parts)]
    last = [send(second[p], dims[(p + 2) % 3]) for p in range(parts)]
    begin = [q_own] + near + second
    other = flash(q_other, begin, None, False, False)
    mine = flash(q_own, begin, None, True, False)
    other = flash(q_other, third, other, False, False)
    mine = flash(q_own, third, mine, True, False)
    partial = flash(q_other, last, other, False, True)
    mine = flash(q_own, last, mine, True, False)
    theirs = send(partial, swap)
    answers = pl.pallas_call(
        combine_kernel,
        out_shape=jax.ShapeDtypeStruct((8, packet_rows, width), bf16),
        in_specs=vmem_specs(4),
        out_specs=vmem_specs(1)[0],
        compiler_params=params,
        name="combine",
    )(*mine, theirs)
    back = lax.all_to_all(answers, axes, 0, 0, axis_index_groups=groups, tiled=True)
    neighbours, log_mass = pl.pallas_call(
        final_kernel,
        out_shape=[
            jax.ShapeDtypeStruct((rows, width), bf16),
            jax.ShapeDtypeStruct((1, rows), f32),
        ],
        in_specs=[smem, smem] + vmem_specs(2),
        out_specs=vmem_specs(2),
        compiler_params=params,
        name="final",
    )(me, cluster_owner, cluster_row, back.reshape(8 * packet_rows, width))
    return neighbours, log_mass.reshape(rows)


def solution(mesh):
    placed = (P(axes, None), P(axes), P())
    dims, swap, groups = links(mesh)
    return jax.shard_map(
        functools.partial(per_device, dims, swap, groups),
        mesh=mesh,
        in_specs=placed,
        out_specs=(P(axes, None), P(axes)),
        check_vma=False,
    )
```

```python
import functools
import math

import jax
import jax.numpy as jnp
from jax import lax
from jax.experimental import pallas as pl
from jax.experimental.pallas import tpu as pltpu
from jax.sharding import PartitionSpec as P

score_scale = 3.0
penalty = 2.0
log2e = math.log2(math.e)
ln2 = math.log(2.0)
masked = -1e30
axes = ("group", "tile")
part_rows = 24
parts = 3
packet_rows = 80
block_keys = 192
block_rows = 208
query_rows = 288
f32 = jnp.float32
bf16 = jnp.bfloat16


def vmem_specs(count):
    return [pl.BlockSpec(memory_space=pltpu.VMEM) for _ in range(count)]


params = pltpu.CompilerParams(vmem_limit_bytes=32 * 1024 * 1024)


def row_facts(clusters_ref, owner_ref, me):
    cluster = clusters_ref[...]
    rows = cluster.shape[1]
    group = jnp.zeros_like(cluster)
    for number in range(owner_ref.shape[0]):
        group = jnp.where(cluster == number, owner_ref[number], group)
    member = lax.broadcasted_iota(jnp.int32, (8, rows), 0) == group
    upper = lax.broadcasted_iota(jnp.int32, (rows, rows), 0) < lax.broadcasted_iota(
        jnp.int32, (rows, rows), 1
    )
    counts = jnp.dot(
        member.astype(f32).astype(bf16), upper.astype(f32).astype(bf16), preferred_element_type=f32
    )
    rank = jnp.sum(jnp.where(member, counts, 0.0), axis=0, keepdims=True).astype(jnp.int32)
    part = (rank >= part_rows).astype(jnp.int32) + (rank >= 2 * part_rows).astype(jnp.int32)
    lane = me * part_rows + rank - part * part_rows
    return cluster, group, rank, part, lane


def hits(count, target):
    shape = (count, target.shape[1])
    return lax.broadcasted_iota(jnp.int32, shape, 0) == target


def ones_at(count, target):
    return hits(count, target).astype(f32).astype(bf16)


def place_kernel(me_ref, owner_ref, clusters_ref, rows_ref, out_ref):
    cluster, group, rank, part, lane = row_facts(clusters_ref, owner_ref, me_ref[0])
    width = rows_ref.shape[1]
    total = out_ref.shape[0]
    placed = jnp.dot(
        ones_at(total, group * packet_rows + rank), rows_ref[...], preferred_element_type=f32
    )
    labels = jnp.where(hits(64, group * 8 + part), (cluster + 1).astype(f32), 0.0).astype(bf16)
    ids = lax.dot_general(
        labels, ones_at(width, lane), (((1,), (1,)), ((), ())), preferred_element_type=f32
    ).astype(bf16)
    source = lax.broadcasted_iota(jnp.int32, (1, 64), 1)
    placed_ids = jnp.dot(
        ones_at(total, (source // 8) * packet_rows + 72 + source % 8), ids, preferred_element_type=f32
    )
    out_ref[...] = (placed + placed_ids).astype(bf16)


def pack_kernel(in_ref, q_ref, big_ref, small_ref):
    packets = [in_ref[s].astype(f32) for s in range(8)]
    for p in range(parts):
        rows = [packets[s][p * part_rows : (p + 1) * part_rows] for s in range(8)]
        ids = packets[0][72:80]
        for s in range(1, 8):
            ids = ids + packets[s][72:80]
        at = lax.broadcasted_iota(jnp.int32, ids.shape, 0)
        row = jnp.sum(jnp.where(at == p, ids, 0.0), axis=0, keepdims=True)
        tail = jnp.where(at == 0, row, 0.0)
        block = jnp.concatenate(rows + [tail, jnp.zeros_like(tail)], axis=0).astype(bf16)
        at = slice(p * block_rows, (p + 1) * block_rows)
        q_ref[at, :] = block
        if p < 2:
            big_ref[at, :] = block
        else:
            small_ref[...] = block


def column_of(row):
    count = block_keys
    wide = row.shape[1]
    eye = lax.broadcasted_iota(jnp.int32, (count, wide), 0) == lax.broadcasted_iota(
        jnp.int32, (count, wide), 1
    )
    return jnp.sum(jnp.where(eye, row, 0.0), axis=1, keepdims=True)


def row_of(column, wide):
    count = column.shape[0]
    eye = lax.broadcasted_iota(jnp.int32, (count, wide), 0) == lax.broadcasted_iota(
        jnp.int32, (count, wide), 1
    )
    return jnp.sum(jnp.where(eye, column, 0.0), axis=0, keepdims=True)


def high_low(value):
    high = value.astype(bf16).astype(f32)
    return high, value - high


def gather_keys(key_refs, blocks, keys):
    id_rows = []
    number = 0
    for ref, count in zip(key_refs, blocks):
        for b in range(count):
            keys[number * block_keys : (number + 1) * block_keys, :] = ref[
                b * block_rows : b * block_rows + block_keys, :
            ]
            ids = ref[b * block_rows + block_keys : (b + 1) * block_rows, 0:256].astype(f32)
            id_rows.append(ids[0:8])
            number += 1
    pieces = []
    for b in range(0, number, 2):
        even = id_rows[b]
        odd = pltpu.roll(id_rows[b + 1], 64, 1)
        pieces += [even[:, 0:128], even[:, 128:256] + odd[:, 0:128], odd[:, 128:256]]
    return jnp.concatenate(pieces, axis=1)[0:1]


def flash_kernel(blocks, first, owns, finish, *refs):
    refs = list(refs)
    count = len(owns)
    q_refs = [refs.pop(0) for _ in range(count)]
    key_refs = [refs.pop(0) for _ in blocks]
    states = None if first else [[refs.pop(0) for _ in range(3)] for _ in range(count)]
    outs = [[refs.pop(0)] if finish else [refs.pop(0) for _ in range(3)] for _ in range(count)]
    keys, queries, labels = refs
    width = q_refs[0].shape[1]
    scale = score_scale / math.sqrt(width) * log2e
    key_id = gather_keys(key_refs, blocks, keys)
    other = jnp.where(key_id == 0.0, masked, -penalty * log2e)
    for n in range(count):
        for p in range(parts):
            at = slice(p * block_keys, (p + 1) * block_keys)
            queries[n, at, :] = q_refs[n][p * block_rows : p * block_rows + block_keys, :]
            ids = q_refs[n][p * block_rows + block_keys : (p + 1) * block_rows, 0:256]
            labels[n, at, :] = column_of(ids.astype(f32)[0:1])
    for n in range(count):
        for start in range(0, parts * block_keys, query_rows):
            at = slice(start, start + query_rows)
            scores = lax.dot_general(
                queries[n, at, :], keys[...], (((1,), (1,)), ((), ())), preferred_element_type=f32
            )
            scores = scores * scale + jnp.where(key_id == labels[n, at, :], 0.0, other)
            if first and owns[n]:
                row = lax.broadcasted_iota(jnp.int32, scores.shape, 0) + start
                scores = jnp.where(
                    row == lax.broadcasted_iota(jnp.int32, scores.shape, 1), masked, scores
                )
            highest = jnp.max(scores, axis=1, keepdims=True)
            if first:
                peak = jnp.maximum(highest, 0.0)
            else:
                former = states[n][0][at, :]
                peak = jnp.maximum(former, highest)
                fade = jnp.exp2(former - peak)
            weights = jnp.exp2(scores - peak)
            mass = jnp.sum(weights, axis=1, keepdims=True)
            acc = jnp.dot(weights.astype(bf16), keys[...], preferred_element_type=f32)
            if not first:
                mass = mass + states[n][1][at, :] * fade
                acc = acc + states[n][2][at, :] * fade
            elif owns[n]:
                mass = mass + jnp.exp2(-peak)
            if not finish:
                outs[n][0][at, :], outs[n][1][at, :], outs[n][2][at, :] = peak, mass, acc
                continue
            safe = jnp.where(mass > 0.0, mass, 1.0)
            outs[n][0][at, :] = (acc / safe).astype(bf16)
            labels[n, at, :] = jnp.where(mass > 0.0, peak + jnp.log2(safe), masked)
    if finish:
        rows = parts * block_keys
        for n in range(count):
            here = lax.broadcasted_iota(jnp.int32, (16, width), 0)
            tails = jnp.zeros((16, width), f32)
            for p in range(parts):
                high, low = high_low(labels[n, p * block_keys : (p + 1) * block_keys, :])
                tails = tails + jnp.where(here == 2 * p, row_of(high, width), 0.0)
                tails = tails + jnp.where(here == 2 * p + 1, row_of(low, width), 0.0)
            outs[n][0][rows : rows + 16, :] = tails.astype(bf16)


def flash(qs, owns, key_arrays, states, finish):
    width = qs[0].shape[1]
    blocks = [a.shape[0] // block_rows for a in key_arrays]
    total = sum(blocks) * block_keys
    rows = parts * block_keys
    first = states is None
    if finish:
        each = [jax.ShapeDtypeStruct((rows + 16, width), bf16)]
    else:
        each = [
            jax.ShapeDtypeStruct((rows, 1), f32),
            jax.ShapeDtypeStruct((rows, 1), f32),
            jax.ShapeDtypeStruct((rows, width), f32),
        ]
    count = len(qs)
    args = [*qs, *key_arrays] + ([] if first else [a for state in states for a in state])
    out = pl.pallas_call(
        functools.partial(flash_kernel, blocks, first, owns, finish),
        out_shape=each * count,
        in_specs=vmem_specs(len(args)),
        out_specs=vmem_specs(len(each) * count),
        scratch_shapes=[
            pltpu.VMEM((total, width), bf16),
            pltpu.VMEM((count, rows, width), bf16),
            pltpu.VMEM((count, rows, 1), f32),
        ],
        compiler_params=params,
        cost_estimate=pl.CostEstimate(
            flops=8 * count * rows * total * width,
            transcendentals=count * rows * total,
            bytes_accessed=2 * total * width + 6 * count * rows * width,
        ),
        name="flash",
    )(*args)
    if finish:
        return out
    return [tuple(out[3 * n : 3 * n + 3]) for n in range(count)]


def combine_kernel(m_ref, l_ref, acc_ref, other_ref, out_ref):
    width = acc_ref.shape[1]
    rows = parts * block_keys
    tails = other_ref[rows : rows + 16, :].astype(f32)
    mixes, levels = [], []
    here = lax.broadcasted_iota(jnp.int32, (8, width), 0)
    for p in range(parts):
        at = slice(p * block_keys, (p + 1) * block_keys)
        level = column_of(
            tails[2 * p : 2 * p + 1, 0:256] + tails[2 * p + 1 : 2 * p + 2, 0:256]
        )
        peak = jnp.maximum(m_ref[at, :], level)
        mine = jnp.exp2(m_ref[at, :] - peak)
        theirs = jnp.exp2(level - peak)
        total = l_ref[at, :] * mine + theirs
        mixes.append(
            (acc_ref[at, :] * mine + other_ref[at, :].astype(f32) * theirs) / total
        )
        high, low = high_low((peak + jnp.log2(total)) * ln2)
        tail = jnp.where(here == p, row_of(high, width), 0.0) + jnp.where(
            here == 3 + p, row_of(low, width), 0.0
        )
        levels = tail if p == 0 else levels + tail
    for s in range(8):
        pieces = [m[s * part_rows : (s + 1) * part_rows] for m in mixes] + [levels]
        out_ref[s] = jnp.concatenate(pieces, axis=0).astype(bf16)


def final_kernel(me_ref, owner_ref, clusters_ref, back_ref, rows_ref, mass_ref):
    _, group, rank, part, lane = row_facts(clusters_ref, owner_ref, me_ref[0])
    total = back_ref.shape[0]
    rows_ref[...] = lax.dot_general(
        ones_at(total, group * packet_rows + rank),
        back_ref[...],
        (((0,), (0,)), ((), ())),
        preferred_element_type=f32,
    ).astype(bf16)
    levels = jnp.concatenate(
        [
            back_ref[g * packet_rows + 64 : (g + 1) * packet_rows, 0:256].astype(f32)[8:16]
            for g in range(8)
        ],
        axis=0,
    ).astype(bf16)
    found = jnp.dot(levels, ones_at(256, lane), preferred_element_type=f32)
    chosen = hits(64, group * 8 + part) | hits(64, group * 8 + 3 + part)
    mass_ref[...] = jnp.sum(jnp.where(chosen, found, 0.0), axis=0, keepdims=True)


def links(mesh):
    side = 4

    def number(y, c, x, z):
        return ((y * 2 + c) * side + x) * side + z

    places = [
        (y, c, x, z) for y in range(side) for c in range(2) for x in range(side) for z in range(side)
    ]

    def pairs(move):
        return [(number(*at), number(*move(*at))) for at in places]

    dims = [
        pairs(lambda y, c, x, z: (y, c, x ^ 3, z)),
        pairs(lambda y, c, x, z: (y, c, x, z ^ 1)),
        pairs(lambda y, c, x, z: (y, c, x, z ^ 3)),
    ]
    swap = pairs(lambda y, c, x, z: (y, c ^ 1, x, z))
    groups = []
    for c in range(2):
        for half in range(2):
            for z in range(side):
                groups.append(
                    [
                        number(y, c, 2 * half + (kind ^ half), z)
                        for y in range(side)
                        for kind in range(2)
                    ]
                )
    return dims, swap, groups


def per_device(dims, swap, groups, embeddings, clusters, cluster_owner):
    rows, width = embeddings.shape
    send = lambda a, pairs: lax.ppermute(a, axes, pairs)
    group_axis, tile = lax.axis_index("group"), lax.axis_index("tile")
    x = tile // 4
    kind = ((x + 1) // 2) % 2
    me = ((group_axis // 2) * 2 + kind).astype(jnp.int32).reshape(1)
    cluster_row = clusters.reshape(1, rows)
    smem = pl.BlockSpec(memory_space=pltpu.SMEM)
    packets = pl.pallas_call(
        place_kernel,
        out_shape=jax.ShapeDtypeStruct((8 * packet_rows, width), bf16),
        in_specs=[smem, smem] + vmem_specs(2),
        out_specs=vmem_specs(1)[0],
        compiler_params=params,
        name="place",
    )(me, cluster_owner, cluster_row, embeddings)
    arrived = lax.all_to_all(
        packets.reshape(8, packet_rows, width), axes, 0, 0, axis_index_groups=groups, tiled=True
    )
    q_own, big, small = pl.pallas_call(
        pack_kernel,
        out_shape=[
            jax.ShapeDtypeStruct((count * block_rows, width), bf16) for count in (parts, 2, 1)
        ],
        in_specs=vmem_specs(1),
        out_specs=vmem_specs(3),
        compiler_params=params,
        name="pack",
    )(arrived)
    wide = [
        [pair for pair in dims[s % 3] if pair[0] // 16 % 2 == 0]
        + [pair for pair in dims[(s + 1) % 3] if pair[0] // 16 % 2 == 1]
        for s in range(3)
    ]
    narrow = [dims[(s + 2) % 3] for s in range(3)]
    big0, small0 = send(big, wide[0]), send(small, narrow[0])
    q_other = send(q_own, swap)
    big0, small0 = lax.optimization_barrier((big0, small0))
    big, small = jnp.concatenate([big, big0], axis=0), jnp.concatenate([small, small0], axis=0)
    big1, small1 = send(big, wide[1]), send(small, narrow[1])
    big2, small2 = send(big, wide[2]), send(small, narrow[2])
    queries, owns = [q_other, q_own], [False, True]
    states = flash(queries, owns, [q_own, big0, small0], None, False)
    big1, small1, states[1] = lax.optimization_barrier((big1, small1, states[1]))
    big3, small3 = send(big1, wide[2]), send(small1, narrow[2])
    states = flash(queries, owns, [big1, small1], states, False)
    states = flash(queries, owns, [big2, small2], states, False)
    (partial,) = flash(queries[:1], owns[:1], [big3, small3], states[:1], True)
    (mine,) = flash(queries[1:], owns[1:], [big3, small3], states[1:], False)
    theirs = send(partial, swap)
    answers = pl.pallas_call(
        combine_kernel,
        out_shape=jax.ShapeDtypeStruct((8, packet_rows, width), bf16),
        in_specs=vmem_specs(4),
        out_specs=vmem_specs(1)[0],
        compiler_params=params,
        name="combine",
    )(*mine, theirs)
    back = lax.all_to_all(answers, axes, 0, 0, axis_index_groups=groups, tiled=True)
    neighbours, log_mass = pl.pallas_call(
        final_kernel,
        out_shape=[
            jax.ShapeDtypeStruct((rows, width), bf16),
            jax.ShapeDtypeStruct((1, rows), f32),
        ],
        in_specs=[smem, smem] + vmem_specs(2),
        out_specs=vmem_specs(2),
        compiler_params=params,
        name="final",
    )(me, cluster_owner, cluster_row, back.reshape(8 * packet_rows, width))
    return neighbours, log_mass.reshape(rows)


def solution(mesh):
    placed = (P(axes, None), P(axes), P())
    dims, swap, groups = links(mesh)
    return jax.shard_map(
        functools.partial(per_device, dims, swap, groups),
        mesh=mesh,
        in_specs=placed,
        out_specs=(P(axes, None), P(axes)),
        check_vma=False,
    )
```

```python
import functools
import math

import jax
import jax.numpy as jnp
from jax import lax
from jax.experimental import pallas as pl
from jax.experimental.pallas import tpu as pltpu
from jax.sharding import PartitionSpec as P

score_scale = 3.0
penalty = 2.0
log2e = math.log2(math.e)
ln2 = math.log(2.0)
masked = -1e30
axes = ("group", "tile")
parts = 3
filled = 72
packet_rows = 80
block_keys = 192
block_rows = 208
query_rows = 288
f32 = jnp.float32
bf16 = jnp.bfloat16


def vmem_specs(count):
    return [pl.BlockSpec(memory_space=pltpu.VMEM) for _ in range(count)]


params = pltpu.CompilerParams(vmem_limit_bytes=32 * 1024 * 1024)


def row_facts(cluster, owner_ref, me):
    rows = cluster.shape[1]
    group = jnp.zeros_like(cluster)
    for number in range(owner_ref.shape[0]):
        group = jnp.where(cluster == number, owner_ref[number], group)
    member = lax.broadcasted_iota(jnp.int32, (8, rows), 0) == group
    upper = lax.broadcasted_iota(jnp.int32, (rows, rows), 0) < lax.broadcasted_iota(
        jnp.int32, (rows, rows), 1
    )
    counts = jnp.dot(
        member.astype(f32).astype(bf16), upper.astype(f32).astype(bf16), preferred_element_type=f32
    )
    rank = jnp.sum(jnp.where(member, counts, 0.0), axis=0, keepdims=True).astype(jnp.int32)
    change = group ^ me
    packet = jnp.where(change == 3, 4, jnp.where(change == 4, 3, change))
    slot = packet * filled + rank
    part = (slot >= block_keys).astype(jnp.int32) + (slot >= 2 * block_keys).astype(jnp.int32)
    return cluster, packet, rank, part, slot - part * block_keys


def hits(count, target):
    shape = (count, target.shape[1])
    return lax.broadcasted_iota(jnp.int32, shape, 0) == target


def ones_at(count, target):
    return hits(count, target).astype(f32).astype(bf16)


def place_kernel(me_ref, owner_ref, clusters_ref, rows_ref, *out_refs):
    cluster, packet, rank, part, lane = row_facts(
        clusters_ref[...].reshape(1, clusters_ref.shape[0]), owner_ref, me_ref[0]
    )
    width = rows_ref.shape[1]
    total = 8 * packet_rows
    placed = jnp.dot(
        ones_at(total, packet * packet_rows + rank), rows_ref[...], preferred_element_type=f32
    )
    labels = jnp.where(hits(64, packet * 8 + part), (cluster + 1).astype(f32), 0.0).astype(bf16)
    ids = lax.dot_general(
        labels, ones_at(width, lane), (((1,), (1,)), ((), ())), preferred_element_type=f32
    ).astype(bf16)
    source = lax.broadcasted_iota(jnp.int32, (1, 64), 1)
    placed_ids = jnp.dot(
        ones_at(total, (source // 8) * packet_rows + filled + source % 8),
        ids,
        preferred_element_type=f32,
    )
    both = (placed + placed_ids).astype(bf16)
    for n in range(8):
        out_refs[n][...] = both[n * packet_rows : (n + 1) * packet_rows]


def spans(p):
    found = []
    for n in range(8):
        low = max(p * block_keys, n * filled) - n * filled
        high = min((p + 1) * block_keys, (n + 1) * filled) - n * filled
        if low < high:
            found.append((n, low, high))
    return found


def pack_kernel(blocks, names, *refs):
    packets = {n: ref[...].astype(f32) for n, ref in zip(names, refs)}
    out_ref = refs[-1]
    for k, p in enumerate(blocks):
        rows = [packets[n][low:high] for n, low, high in spans(p)]
        ids = sum(packets[n][filled : filled + 8] for n, _, _ in spans(p))
        at = lax.broadcasted_iota(jnp.int32, ids.shape, 0)
        row = jnp.sum(jnp.where(at == p, ids, 0.0), axis=0, keepdims=True)
        tail = jnp.where(at == 0, row, 0.0)
        out_ref[k * block_rows : (k + 1) * block_rows, :] = jnp.concatenate(
            rows + [tail, jnp.zeros_like(tail)], axis=0
        ).astype(bf16)


def pack(blocks, packets):
    names = sorted({n for p in blocks for n, _, _ in spans(p)})
    width = packets[0].shape[1]
    return pl.pallas_call(
        functools.partial(pack_kernel, blocks, names),
        out_shape=jax.ShapeDtypeStruct((len(blocks) * block_rows, width), bf16),
        in_specs=vmem_specs(len(names)),
        out_specs=vmem_specs(1)[0],
        compiler_params=params,
        name="pack",
    )(*[packets[n] for n in names])


def column_of(row):
    count = block_keys
    wide = row.shape[1]
    eye = lax.broadcasted_iota(jnp.int32, (count, wide), 0) == lax.broadcasted_iota(
        jnp.int32, (count, wide), 1
    )
    return jnp.sum(jnp.where(eye, row, 0.0), axis=1, keepdims=True)


def row_of(column, wide):
    count = column.shape[0]
    eye = lax.broadcasted_iota(jnp.int32, (count, wide), 0) == lax.broadcasted_iota(
        jnp.int32, (count, wide), 1
    )
    return jnp.sum(jnp.where(eye, column, 0.0), axis=0, keepdims=True)


def high_low(value):
    high = value.astype(bf16).astype(f32)
    return high, value - high


def gather_keys(key_refs, blocks, keys):
    id_rows = []
    number = 0
    for ref, count in zip(key_refs, blocks):
        for b in range(count):
            keys[number * block_keys : (number + 1) * block_keys, :] = ref[
                b * block_rows : b * block_rows + block_keys, :
            ]
            ids = ref[b * block_rows + block_keys : (b + 1) * block_rows, 0:256].astype(f32)
            id_rows.append(ids[0:8])
            number += 1
    pieces = []
    for b in range(0, number, 2):
        even = id_rows[b]
        odd = pltpu.roll(id_rows[b + 1], 64, 1)
        pieces += [even[:, 0:128], even[:, 128:256] + odd[:, 0:128], odd[:, 128:256]]
    return jnp.concatenate(pieces, axis=1)[0:1]


def flash_kernel(blocks, first, owns, finish, *refs):
    refs = list(refs)
    count = len(owns)
    q_refs = [[refs.pop(0), refs.pop(0)] for _ in range(count)]
    key_refs = [refs.pop(0) for _ in blocks]
    states = None if first else [[refs.pop(0) for _ in range(3)] for _ in range(count)]
    outs = [[refs.pop(0)] if finish else [refs.pop(0) for _ in range(3)] for _ in range(count)]
    keys, queries, labels = refs
    width = q_refs[0][0].shape[1]
    scale = score_scale / math.sqrt(width) * log2e
    key_id = gather_keys(key_refs, blocks, keys)
    other = jnp.where(key_id == 0.0, masked, -penalty * log2e)
    for n in range(count):
        for p in range(parts):
            at = slice(p * block_keys, (p + 1) * block_keys)
            ref, first_row = q_refs[n][p // 2], (p % 2) * block_rows
            queries[n, at, :] = ref[first_row : first_row + block_keys, :]
            ids = ref[first_row + block_keys : first_row + block_rows, 0:256]
            labels[n, at, :] = column_of(ids.astype(f32)[0:1])
    for n in range(count):
        for start in range(0, parts * block_keys, query_rows):
            at = slice(start, start + query_rows)
            scores = lax.dot_general(
                queries[n, at, :], keys[...], (((1,), (1,)), ((), ())), preferred_element_type=f32
            )
            scores = scores * scale + jnp.where(key_id == labels[n, at, :], 0.0, other)
            if first and owns[n]:
                row = lax.broadcasted_iota(jnp.int32, scores.shape, 0) + start
                scores = jnp.where(
                    row == lax.broadcasted_iota(jnp.int32, scores.shape, 1), masked, scores
                )
            highest = jnp.max(scores, axis=1, keepdims=True)
            if first:
                peak = jnp.maximum(highest, 0.0)
            else:
                former = states[n][0][at, :]
                peak = jnp.maximum(former, highest)
                fade = jnp.exp2(former - peak)
            weights = jnp.exp2(scores - peak)
            mass = jnp.sum(weights, axis=1, keepdims=True)
            acc = jnp.dot(weights.astype(bf16), keys[...], preferred_element_type=f32)
            if not first:
                mass = mass + states[n][1][at, :] * fade
                acc = acc + states[n][2][at, :] * fade
            elif owns[n]:
                mass = mass + jnp.exp2(-peak)
            if not finish:
                outs[n][0][at, :], outs[n][1][at, :], outs[n][2][at, :] = peak, mass, acc
                continue
            safe = jnp.where(mass > 0.0, mass, 1.0)
            outs[n][0][at, :] = (acc / safe).astype(bf16)
            labels[n, at, :] = jnp.where(mass > 0.0, peak + jnp.log2(safe), masked)
    if finish:
        rows = parts * block_keys
        for n in range(count):
            here = lax.broadcasted_iota(jnp.int32, (16, width), 0)
            tails = jnp.zeros((16, width), f32)
            for p in range(parts):
                high, low = high_low(labels[n, p * block_keys : (p + 1) * block_keys, :])
                tails = tails + jnp.where(here == 2 * p, row_of(high, width), 0.0)
                tails = tails + jnp.where(here == 2 * p + 1, row_of(low, width), 0.0)
            outs[n][0][rows : rows + 16, :] = tails.astype(bf16)


def flash(qs, owns, key_arrays, states, finish):
    width = qs[0][0].shape[1]
    blocks = [a.shape[0] // block_rows for a in key_arrays]
    total = sum(blocks) * block_keys
    rows = parts * block_keys
    first = states is None
    if finish:
        each = [jax.ShapeDtypeStruct((rows + 16, width), bf16)]
    else:
        each = [
            jax.ShapeDtypeStruct((rows, 1), f32),
            jax.ShapeDtypeStruct((rows, 1), f32),
            jax.ShapeDtypeStruct((rows, width), f32),
        ]
    count = len(qs)
    args = [a for q in qs for a in q] + list(key_arrays) + ([] if first else [a for state in states for a in state])
    out = pl.pallas_call(
        functools.partial(flash_kernel, blocks, first, owns, finish),
        out_shape=each * count,
        in_specs=vmem_specs(len(args)),
        out_specs=vmem_specs(len(each) * count),
        scratch_shapes=[
            pltpu.VMEM((total, width), bf16),
            pltpu.VMEM((count, rows, width), bf16),
            pltpu.VMEM((count, rows, 1), f32),
        ],
        compiler_params=params,
        cost_estimate=pl.CostEstimate(
            flops=8 * count * rows * total * width,
            transcendentals=count * rows * total,
            bytes_accessed=2 * total * width + 6 * count * rows * width,
        ),
        name="flash",
    )(*args)
    if finish:
        return out
    return [tuple(out[3 * n : 3 * n + 3]) for n in range(count)]


def combine_kernel(m_ref, l_ref, acc_ref, other_ref, *out_refs):
    width = acc_ref.shape[1]
    rows = parts * block_keys
    tails = other_ref[rows : rows + 16, :].astype(f32)
    mixes, levels = [], []
    here = lax.broadcasted_iota(jnp.int32, (8, width), 0)
    for p in range(parts):
        at = slice(p * block_keys, (p + 1) * block_keys)
        level = column_of(
            tails[2 * p : 2 * p + 1, 0:256] + tails[2 * p + 1 : 2 * p + 2, 0:256]
        )
        peak = jnp.maximum(m_ref[at, :], level)
        mine = jnp.exp2(m_ref[at, :] - peak)
        theirs = jnp.exp2(level - peak)
        total = l_ref[at, :] * mine + theirs
        mixes.append(
            (acc_ref[at, :] * mine + other_ref[at, :].astype(f32) * theirs) / total
        )
        high, low = high_low((peak + jnp.log2(total)) * ln2)
        tail = jnp.where(here == p, row_of(high, width), 0.0) + jnp.where(
            here == 3 + p, row_of(low, width), 0.0
        )
        levels = tail if p == 0 else levels + tail
    for n in range(8):
        pieces = [
            mixes[p][n * filled + low - p * block_keys : n * filled + high - p * block_keys]
            for p in range(parts)
            for other, low, high in spans(p)
            if other == n
        ]
        out_refs[n][...] = jnp.concatenate(pieces + [levels], axis=0).astype(bf16)


def final_kernel(me_ref, owner_ref, clusters_ref, *refs):
    backs, (rows_ref, mass_ref, back) = refs[:8], refs[8:]
    _, packet, rank, part, lane = row_facts(
        clusters_ref[...].reshape(1, clusters_ref.shape[0]), owner_ref, me_ref[0]
    )
    for n in range(8):
        back[n * packet_rows : (n + 1) * packet_rows, :] = backs[n][...]
    rows_ref[...] = lax.dot_general(
        ones_at(8 * packet_rows, packet * packet_rows + rank),
        back[...],
        (((0,), (0,)), ((), ())),
        preferred_element_type=f32,
    ).astype(bf16)
    levels = jnp.concatenate(
        [backs[n][64:packet_rows, 0:256].astype(f32)[8:16] for n in range(8)], axis=0
    ).astype(bf16)
    found = jnp.dot(levels, ones_at(256, lane), preferred_element_type=f32)
    chosen = hits(64, packet * 8 + part) | hits(64, packet * 8 + 3 + part)
    mass_ref[...] = jnp.sum(jnp.where(chosen, found, 0.0), axis=0, keepdims=True).reshape(
        mass_ref.shape
    )


def links(mesh):
    side = 4

    def number(y, c, x, z):
        return ((y * 2 + c) * side + x) * side + z

    places = [
        (y, c, x, z) for y in range(side) for c in range(2) for x in range(side) for z in range(side)
    ]

    def pairs(move):
        return [(number(*at), number(*move(*at))) for at in places]

    dims = [
        pairs(lambda y, c, x, z: (y, c, x ^ 3, z)),
        pairs(lambda y, c, x, z: (y ^ 3, c, x, z)),
        pairs(lambda y, c, x, z: (y, c, x, z ^ 3)),
    ]
    swap = pairs(lambda y, c, x, z: (y, c ^ 1, x, z))
    trips = [
        pairs(lambda y, c, x, z, m=m: (y ^ (m >> 1 & 1), c, x ^ (m & 1), z ^ (m >> 2)))
        for m in (0, 1, 2, 4, 3, 5, 6, 7)
    ]
    return dims, swap, trips


def per_device(dims, swap, trips, embeddings, clusters, cluster_owner):
    rows, width = embeddings.shape
    send = lambda a, pairs: lax.ppermute(a, axes, pairs)
    group_axis, tile = lax.axis_index("group"), lax.axis_index("tile")
    kind = lambda at: (at + 1) // 2 % 2
    me = kind(tile // 4) + 2 * kind(group_axis // 2) + 4 * kind(tile % 4)
    me = me.astype(jnp.int32).reshape(1)
    smem = pl.BlockSpec(memory_space=pltpu.SMEM)
    packet = jax.ShapeDtypeStruct((packet_rows, width), bf16)
    packets = pl.pallas_call(
        place_kernel,
        out_shape=[packet] * 8,
        in_specs=[smem, smem] + vmem_specs(2),
        out_specs=vmem_specs(8),
        compiler_params=params,
        name="place",
    )(me, cluster_owner, clusters, embeddings)
    arrived = [packets[0]] + [send(packets[n], trips[n]) for n in range(1, 8)]
    big, small = pack((0, 1), arrived), pack((2,), arrived)
    wide = [
        [pair for pair in dims[s % 3] if pair[0] // 16 % 2 == 0]
        + [pair for pair in dims[(s + 1) % 3] if pair[0] // 16 % 2 == 1]
        for s in range(3)
    ]
    narrow = [dims[(s + 2) % 3] for s in range(3)]
    big0, small0 = send(big, wide[0]), send(small, narrow[0])
    q_own, q_other = (big, small), (send(big, swap), send(small, swap))
    big0, small0 = lax.optimization_barrier((big0, small0))
    big, small = jnp.concatenate([big, big0], axis=0), jnp.concatenate([small, small0], axis=0)
    big1, small1 = send(big, wide[1]), send(small, narrow[1])
    big2, small2 = send(big, wide[2]), send(small, narrow[2])
    queries, owns = [q_other, q_own], [False, True]
    states = flash(queries, owns, [*q_own, big0, small0], None, False)
    big1, small1, states[1] = lax.optimization_barrier((big1, small1, states[1]))
    big3, small3 = send(big1, wide[2]), send(small1, narrow[2])
    states = flash(queries, owns, [big1, small1], states, False)
    states = flash(queries, owns, [big2, small2], states, False)
    (partial,) = flash(queries[:1], owns[:1], [big3, small3], states[:1], True)
    (mine,) = flash(queries[1:], owns[1:], [big3, small3], states[1:], False)
    theirs = send(partial, swap)
    answers = pl.pallas_call(
        combine_kernel,
        out_shape=[packet] * 8,
        in_specs=vmem_specs(4),
        out_specs=vmem_specs(8),
        compiler_params=params,
        name="combine",
    )(*mine, theirs)
    back = [answers[0]] + [send(answers[n], trips[n]) for n in range(1, 8)]
    neighbours, log_mass = pl.pallas_call(
        final_kernel,
        out_shape=[jax.ShapeDtypeStruct((rows, width), bf16), jax.ShapeDtypeStruct((rows,), f32)],
        in_specs=[smem, smem] + vmem_specs(9),
        out_specs=vmem_specs(2),
        scratch_shapes=[pltpu.VMEM((8 * packet_rows, width), bf16)],
        compiler_params=params,
        name="final",
    )(me, cluster_owner, clusters, *back)
    return neighbours, log_mass


def solution(mesh):
    placed = (P(axes, None), P(axes), P())
    dims, swap, trips = links(mesh)
    return jax.shard_map(
        functools.partial(per_device, dims, swap, trips),
        mesh=mesh,
        in_specs=placed,
        out_specs=(P(axes, None), P(axes)),
        check_vma=False,
    )
```

```python
import functools
import math

import jax
import jax.numpy as jnp
from jax import lax
from jax.experimental import pallas as pl
from jax.experimental.pallas import tpu as pltpu
from jax.sharding import PartitionSpec as P

score_scale = 3.0
penalty = 2.0
log2e = math.log2(math.e)
ln2 = math.log(2.0)
masked = -1e30
axes = ("group", "tile")
parts = 3
filled = 72
packet_rows = 80
block_keys = 192
big_rows = 400
small_rows = 200
query_rows = 288
f32 = jnp.float32
bf16 = jnp.bfloat16


def vmem_specs(count):
    return [pl.BlockSpec(memory_space=pltpu.VMEM) for _ in range(count)]


params = pltpu.CompilerParams(vmem_limit_bytes=32 * 1024 * 1024)


def row_facts(cluster, owner_ref, me):
    rows = cluster.shape[1]
    group = jnp.zeros_like(cluster)
    for number in range(owner_ref.shape[0]):
        group = jnp.where(cluster == number, owner_ref[number], group)
    member = lax.broadcasted_iota(jnp.int32, (8, rows), 0) == group
    upper = lax.broadcasted_iota(jnp.int32, (rows, rows), 0) < lax.broadcasted_iota(
        jnp.int32, (rows, rows), 1
    )
    counts = jnp.dot(
        member.astype(f32).astype(bf16), upper.astype(f32).astype(bf16), preferred_element_type=f32
    )
    rank = jnp.sum(jnp.where(member, counts, 0.0), axis=0, keepdims=True).astype(jnp.int32)
    change = group ^ me
    packet = jnp.where(change == 3, 4, jnp.where(change == 4, 3, change))
    slot = packet * filled + rank
    part = (slot >= block_keys).astype(jnp.int32) + (slot >= 2 * block_keys).astype(jnp.int32)
    return cluster, packet, rank, part, slot - part * block_keys


def hits(count, target):
    shape = (count, target.shape[1])
    return lax.broadcasted_iota(jnp.int32, shape, 0) == target


def ones_at(count, target):
    return hits(count, target).astype(f32).astype(bf16)


def place_kernel(me_ref, owner_hbm, clusters_hbm, rows_hbm, *refs):
    out_refs, (owner_ref, clusters_ref, rows_ref, done) = refs[:8], refs[8:]
    copies = [
        pltpu.make_async_copy(source, target, done.at[n])
        for n, (source, target) in enumerate(
            ((owner_hbm, owner_ref), (clusters_hbm, clusters_ref), (rows_hbm, rows_ref))
        )
    ]
    for copy in copies:
        copy.start()
    copies[0].wait()
    copies[1].wait()
    cluster, packet, rank, part, lane = row_facts(
        clusters_ref[...].reshape(1, clusters_ref.shape[0]), owner_ref, me_ref[0]
    )
    width = rows_ref.shape[1]
    total = 8 * packet_rows
    copies[2].wait()
    placed = jnp.dot(
        ones_at(total, packet * packet_rows + rank), rows_ref[...], preferred_element_type=f32
    )
    labels = jnp.where(hits(64, packet * 8 + part), (cluster + 1).astype(f32), 0.0).astype(bf16)
    ids = lax.dot_general(
        labels, ones_at(width, lane), (((1,), (1,)), ((), ())), preferred_element_type=f32
    ).astype(bf16)
    source = lax.broadcasted_iota(jnp.int32, (1, 64), 1)
    placed_ids = jnp.dot(
        ones_at(total, (source // 8) * packet_rows + filled + source % 8),
        ids,
        preferred_element_type=f32,
    )
    both = (placed + placed_ids).astype(bf16)
    for n in range(8):
        out_refs[n][...] = both[n * packet_rows : (n + 1) * packet_rows]


def spans(p):
    found = []
    for n in range(8):
        low = max(p * block_keys, n * filled) - n * filled
        high = min((p + 1) * block_keys, (n + 1) * filled) - n * filled
        if low < high:
            found.append((n, low, high))
    return found


def pack_kernel(*refs):
    packets = [ref[...].astype(f32) for ref in refs[:8]]
    big_ref, small_ref = refs[8:]
    blocks = [
        jnp.concatenate([packets[n][low:high] for n, low, high in spans(p)], axis=0)
        for p in range(parts)
    ]
    ids = sum(packet[filled:packet_rows] for packet in packets)
    at = lax.broadcasted_iota(jnp.int32, ids.shape, 0)
    big_ref[0 : 2 * block_keys, :] = jnp.concatenate(blocks[:2], axis=0).astype(bf16)
    big_ref[2 * block_keys : big_rows, :] = jnp.concatenate(
        [jnp.where(at < 2, ids, 0.0), jnp.zeros_like(ids)], axis=0
    ).astype(bf16)
    last = jnp.sum(jnp.where(at == 2, ids, 0.0), axis=0, keepdims=True)
    small_ref[...] = jnp.concatenate([blocks[2], jnp.where(at == 0, last, 0.0)], axis=0).astype(bf16)


def pack(packets):
    width = packets[0].shape[1]
    return pl.pallas_call(
        pack_kernel,
        out_shape=[jax.ShapeDtypeStruct((count, width), bf16) for count in (big_rows, small_rows)],
        in_specs=vmem_specs(8),
        out_specs=vmem_specs(2),
        compiler_params=params,
        name="pack",
    )(*packets)


def column_of(row):
    count = block_keys
    wide = row.shape[1]
    eye = lax.broadcasted_iota(jnp.int32, (count, wide), 0) == lax.broadcasted_iota(
        jnp.int32, (count, wide), 1
    )
    return jnp.sum(jnp.where(eye, row, 0.0), axis=1, keepdims=True)


def row_of(column, wide):
    count = column.shape[0]
    eye = lax.broadcasted_iota(jnp.int32, (count, wide), 0) == lax.broadcasted_iota(
        jnp.int32, (count, wide), 1
    )
    return jnp.sum(jnp.where(eye, column, 0.0), axis=0, keepdims=True)


def high_low(value):
    high = value.astype(bf16).astype(f32)
    return high, value - high


def gather_rows(refs, wides, store):
    id_rows = []
    for ref, wide in zip(refs, wides):
        step, count = (big_rows, 2) if wide else (small_rows, 1)
        for start in range(0, ref.shape[0], step):
            end = start + count * block_keys
            first = len(id_rows) * block_keys
            store[first : first + count * block_keys, :] = ref[start:end, :]
            ids = ref[end : end + 8 * count, 0:256].astype(f32)[0:8]
            id_rows += [ids, pltpu.roll(ids, 7, 0)][:count]
    return id_rows


def side_by_side(id_rows):
    pieces = []
    for even, odd in zip(id_rows[::2], id_rows[1::2]):
        odd = pltpu.roll(odd, 64, 1)
        pieces += [even[:, 0:128], even[:, 128:256] + odd[:, 0:128], odd[:, 128:256]]
    return jnp.concatenate(pieces, axis=1)[0:1]


def flash_kernel(wides, first, owns, finish, *refs):
    refs = list(refs)
    count = len(owns)
    q_refs = [[refs.pop(0), refs.pop(0)] for _ in range(count)]
    key_refs = [refs.pop(0) for _ in wides]
    states = None if first else [[refs.pop(0) for _ in range(3)] for _ in range(count)]
    outs = [[refs.pop(0)] if finish else [refs.pop(0) for _ in range(3)] for _ in range(count)]
    keys, queries, labels = refs
    width = q_refs[0][0].shape[1]
    scale = score_scale / math.sqrt(width) * log2e
    key_id = side_by_side(gather_rows(key_refs, wides, keys))
    other = jnp.where(key_id == 0.0, masked, -penalty * log2e)
    for n in range(count):
        for p, ids in enumerate(gather_rows(q_refs[n], (True, False), queries.at[n])):
            labels[n, p * block_keys : (p + 1) * block_keys, :] = column_of(ids[0:1])
    for n in range(count):
        for start in range(0, parts * block_keys, query_rows):
            at = slice(start, start + query_rows)
            scores = lax.dot_general(
                queries[n, at, :], keys[...], (((1,), (1,)), ((), ())), preferred_element_type=f32
            )
            scores = scores * scale + jnp.where(key_id == labels[n, at, :], 0.0, other)
            if first and owns[n]:
                row = lax.broadcasted_iota(jnp.int32, scores.shape, 0) + start
                scores = jnp.where(
                    row == lax.broadcasted_iota(jnp.int32, scores.shape, 1), masked, scores
                )
            highest = jnp.max(scores, axis=1, keepdims=True)
            if first:
                peak = jnp.maximum(highest, 0.0)
            else:
                former = states[n][0][at, :]
                peak = jnp.maximum(former, highest)
                fade = jnp.exp2(former - peak)
            weights = jnp.exp2(scores - peak)
            mass = jnp.sum(weights, axis=1, keepdims=True)
            acc = jnp.dot(weights.astype(bf16), keys[...], preferred_element_type=f32)
            if not first:
                mass = mass + states[n][1][at, :] * fade
                acc = acc + states[n][2][at, :] * fade
            elif owns[n]:
                mass = mass + jnp.exp2(-peak)
            if not finish:
                outs[n][0][at, :], outs[n][1][at, :], outs[n][2][at, :] = peak, mass, acc
                continue
            safe = jnp.where(mass > 0.0, mass, 1.0)
            outs[n][0][at, :] = (acc / safe).astype(bf16)
            labels[n, at, :] = jnp.where(mass > 0.0, peak + jnp.log2(safe), masked)
    if finish:
        rows = parts * block_keys
        for n in range(count):
            here = lax.broadcasted_iota(jnp.int32, (16, width), 0)
            tails = jnp.zeros((16, width), f32)
            for p in range(parts):
                high, low = high_low(labels[n, p * block_keys : (p + 1) * block_keys, :])
                tails = tails + jnp.where(here == 2 * p, row_of(high, width), 0.0)
                tails = tails + jnp.where(here == 2 * p + 1, row_of(low, width), 0.0)
            outs[n][0][rows : rows + 16, :] = tails.astype(bf16)


def flash(qs, owns, key_arrays, states, finish):
    width = qs[0][0].shape[1]
    wides = [wide for _, wide in key_arrays]
    key_arrays = [a for a, _ in key_arrays]
    total = sum(
        a.shape[0] // big_rows * 2 if wide else a.shape[0] // small_rows
        for a, wide in zip(key_arrays, wides)
    )
    total *= block_keys
    rows = parts * block_keys
    first = states is None
    if finish:
        each = [jax.ShapeDtypeStruct((rows + 16, width), bf16)]
    else:
        each = [
            jax.ShapeDtypeStruct((rows, 1), f32),
            jax.ShapeDtypeStruct((rows, 1), f32),
            jax.ShapeDtypeStruct((rows, width), f32),
        ]
    count = len(qs)
    args = [a for q in qs for a in q] + key_arrays + ([] if first else [a for state in states for a in state])
    out = pl.pallas_call(
        functools.partial(flash_kernel, wides, first, owns, finish),
        out_shape=each * count,
        in_specs=vmem_specs(len(args)),
        out_specs=vmem_specs(len(each) * count),
        scratch_shapes=[
            pltpu.VMEM((total, width), bf16),
            pltpu.VMEM((count, rows, width), bf16),
            pltpu.VMEM((count, rows, 1), f32),
        ],
        compiler_params=params,
        cost_estimate=pl.CostEstimate(
            flops=8 * count * rows * total * width,
            transcendentals=count * rows * total,
            bytes_accessed=2 * total * width + 6 * count * rows * width,
        ),
        name="flash",
    )(*args)
    if finish:
        return out
    return [tuple(out[3 * n : 3 * n + 3]) for n in range(count)]


def combine_kernel(m_ref, l_ref, acc_ref, other_ref, *out_refs):
    width = acc_ref.shape[1]
    rows = parts * block_keys
    tails = other_ref[rows : rows + 16, :].astype(f32)
    mixes, levels = [], []
    here = lax.broadcasted_iota(jnp.int32, (8, width), 0)
    for p in range(parts):
        at = slice(p * block_keys, (p + 1) * block_keys)
        level = column_of(
            tails[2 * p : 2 * p + 1, 0:256] + tails[2 * p + 1 : 2 * p + 2, 0:256]
        )
        peak = jnp.maximum(m_ref[at, :], level)
        mine = jnp.exp2(m_ref[at, :] - peak)
        theirs = jnp.exp2(level - peak)
        total = l_ref[at, :] * mine + theirs
        mixes.append(
            (acc_ref[at, :] * mine + other_ref[at, :].astype(f32) * theirs) / total
        )
        high, low = high_low((peak + jnp.log2(total)) * ln2)
        tail = jnp.where(here == p, row_of(high, width), 0.0) + jnp.where(
            here == 3 + p, row_of(low, width), 0.0
        )
        levels = tail if p == 0 else levels + tail
    for n in range(8):
        pieces = [
            mixes[p][n * filled + low - p * block_keys : n * filled + high - p * block_keys]
            for p in range(parts)
            for other, low, high in spans(p)
            if other == n
        ]
        out_refs[n][...] = jnp.concatenate(pieces + [levels], axis=0).astype(bf16)


def final_kernel(me_ref, owner_ref, clusters_ref, *refs):
    backs, (rows_ref, mass_ref, back) = refs[:8], refs[8:]
    _, packet, rank, part, lane = row_facts(
        clusters_ref[...].reshape(1, clusters_ref.shape[0]), owner_ref, me_ref[0]
    )
    for n in range(8):
        back[n * packet_rows : (n + 1) * packet_rows, :] = backs[n][...]
    rows_ref[...] = lax.dot_general(
        ones_at(8 * packet_rows, packet * packet_rows + rank),
        back[...],
        (((0,), (0,)), ((), ())),
        preferred_element_type=f32,
    ).astype(bf16)
    levels = jnp.concatenate(
        [backs[n][64:packet_rows, 0:256].astype(f32)[8:16] for n in range(8)], axis=0
    ).astype(bf16)
    found = jnp.dot(levels, ones_at(256, lane), preferred_element_type=f32)
    chosen = hits(64, packet * 8 + part) | hits(64, packet * 8 + 3 + part)
    mass_ref[...] = jnp.sum(jnp.where(chosen, found, 0.0), axis=0, keepdims=True).reshape(
        mass_ref.shape
    )


def links(mesh):
    side = 4

    def number(y, c, x, z):
        return ((y * 2 + c) * side + x) * side + z

    places = [
        (y, c, x, z) for y in range(side) for c in range(2) for x in range(side) for z in range(side)
    ]

    def pairs(move):
        return [(number(*at), number(*move(*at))) for at in places]

    dims = [
        pairs(lambda y, c, x, z: (y, c, x ^ 3, z)),
        pairs(lambda y, c, x, z: (y ^ 3, c, x, z)),
        pairs(lambda y, c, x, z: (y, c, x, z ^ 3)),
    ]
    swap = pairs(lambda y, c, x, z: (y, c ^ 1, x, z))
    trips = [
        pairs(lambda y, c, x, z, m=m: (y ^ (m >> 1 & 1), c, x ^ (m & 1), z ^ (m >> 2)))
        for m in (0, 1, 2, 4, 3, 5, 6, 7)
    ]
    return dims, swap, trips


def per_device(dims, swap, trips, embeddings, clusters, cluster_owner):
    rows, width = embeddings.shape
    send = lambda a, pairs: lax.ppermute(a, axes, pairs)
    group_axis, tile = lax.axis_index("group"), lax.axis_index("tile")
    kind = lambda at: (at + 1) // 2 % 2
    me = kind(tile // 4) + 2 * kind(group_axis // 2) + 4 * kind(tile % 4)
    me = me.astype(jnp.int32).reshape(1)
    smem = pl.BlockSpec(memory_space=pltpu.SMEM)
    packet = jax.ShapeDtypeStruct((packet_rows, width), bf16)
    packets = pl.pallas_call(
        place_kernel,
        out_shape=[packet] * 8,
        in_specs=[smem] + [pl.BlockSpec(memory_space=pltpu.HBM)] * 3,
        out_specs=vmem_specs(8),
        scratch_shapes=[
            pltpu.SMEM(cluster_owner.shape, jnp.int32),
            pltpu.VMEM(clusters.shape, jnp.int32),
            pltpu.VMEM(embeddings.shape, bf16),
            pltpu.SemaphoreType.DMA((3,)),
        ],
        compiler_params=params,
        name="place",
    )(me, cluster_owner, clusters, embeddings)
    arrived = [packets[0]] + [send(packets[n], trips[n]) for n in range(1, 8)]
    big, small = pack(arrived)
    wide = [
        [pair for pair in dims[s % 3] if pair[0] // 16 % 2 == 0]
        + [pair for pair in dims[(s + 1) % 3] if pair[0] // 16 % 2 == 1]
        for s in range(3)
    ]
    narrow = [dims[(s + 2) % 3] for s in range(3)]
    big0, small0 = send(big, wide[0]), send(small, narrow[0])
    q_own, q_other = (big, small), (send(big, swap), send(small, swap))
    big0, small0 = lax.optimization_barrier((big0, small0))
    big, small = jnp.concatenate([big, big0], axis=0), jnp.concatenate([small, small0], axis=0)
    big1, small1 = send(big, wide[1]), send(small, narrow[1])
    queries, owns = [q_other, q_own], [False, True]
    pairs = lambda *units: list(zip(units, (True, False) * 2))
    states = flash(queries, owns, pairs(*q_own, big0, small0), None, False)
    big, small, states[1] = lax.optimization_barrier((big, small, states[1]))
    big2, small2 = send(big, wide[2]), send(small, narrow[2])
    big3, small3 = send(big1, wide[2]), send(small1, narrow[2])
    states = flash(queries, owns, pairs(big1, small1), states, False)
    states = flash(queries, owns, pairs(big2, small2), states, False)
    (partial,) = flash(queries[:1], owns[:1], pairs(big3, small3), states[:1], True)
    (mine,) = flash(queries[1:], owns[1:], pairs(big3, small3), states[1:], False)
    theirs = send(partial, swap)
    answers = pl.pallas_call(
        combine_kernel,
        out_shape=[packet] * 8,
        in_specs=vmem_specs(4),
        out_specs=vmem_specs(8),
        compiler_params=params,
        name="combine",
    )(*mine, theirs)
    back = [answers[0]] + [send(answers[n], trips[n]) for n in range(1, 8)]
    neighbours, log_mass = pl.pallas_call(
        final_kernel,
        out_shape=[jax.ShapeDtypeStruct((rows, width), bf16), jax.ShapeDtypeStruct((rows,), f32)],
        in_specs=[smem, smem] + vmem_specs(9),
        out_specs=vmem_specs(2),
        scratch_shapes=[pltpu.VMEM((8 * packet_rows, width), bf16)],
        compiler_params=params,
        name="final",
    )(me, cluster_owner, clusters, *back)
    return neighbours, log_mass


def solution(mesh):
    placed = (P(axes, None), P(axes), P())
    dims, swap, trips = links(mesh)
    return jax.shard_map(
        functools.partial(per_device, dims, swap, trips),
        mesh=mesh,
        in_specs=placed,
        out_specs=(P(axes, None), P(axes)),
        check_vma=False,
    )
```

```python
import functools
import math

import jax
import jax.numpy as jnp
from jax import lax
from jax.experimental import pallas as pl
from jax.experimental.pallas import tpu as pltpu
from jax.sharding import PartitionSpec as P

score_scale = 3.0
penalty = 2.0
log2e = math.log2(math.e)
ln2 = math.log(2.0)
masked = -1e30
axes = ("group", "tile")
parts = 3
filled = 72
packet_rows = 80
block_keys = 192
big_rows = 400
small_rows = 200
query_rows = 288
f32 = jnp.float32
bf16 = jnp.bfloat16


def vmem_specs(count):
    return [pl.BlockSpec(memory_space=pltpu.VMEM) for _ in range(count)]


params = pltpu.CompilerParams(vmem_limit_bytes=32 * 1024 * 1024)


def row_facts(cluster, owner_ref, me):
    rows = cluster.shape[1]
    group = jnp.zeros_like(cluster)
    for number in range(owner_ref.shape[0]):
        group = jnp.where(cluster == number, owner_ref[number], group)
    member = lax.broadcasted_iota(jnp.int32, (8, rows), 0) == group
    upper = lax.broadcasted_iota(jnp.int32, (rows, rows), 0) < lax.broadcasted_iota(
        jnp.int32, (rows, rows), 1
    )
    counts = jnp.dot(
        member.astype(f32).astype(bf16), upper.astype(f32).astype(bf16), preferred_element_type=f32
    )
    rank = jnp.sum(jnp.where(member, counts, 0.0), axis=0, keepdims=True).astype(jnp.int32)
    change = group ^ me
    packet = jnp.where(change == 3, 4, jnp.where(change == 4, 3, change))
    slot = packet * filled + rank
    part = (slot >= block_keys).astype(jnp.int32) + (slot >= 2 * block_keys).astype(jnp.int32)
    return cluster, packet, rank, part, slot - part * block_keys


def hits(count, target):
    shape = (count, target.shape[1])
    return lax.broadcasted_iota(jnp.int32, shape, 0) == target


def ones_at(count, target):
    return hits(count, target).astype(f32).astype(bf16)


def place_kernel(me_ref, owner_hbm, clusters_hbm, rows_hbm, *refs):
    out_refs, (owner_ref, clusters_ref, rows_ref, done) = refs[:8], refs[8:]
    copies = [
        pltpu.make_async_copy(source, target, done.at[n])
        for n, (source, target) in enumerate(
            ((owner_hbm, owner_ref), (clusters_hbm, clusters_ref), (rows_hbm, rows_ref))
        )
    ]
    for copy in copies:
        copy.start()
    copies[0].wait()
    copies[1].wait()
    cluster, packet, rank, part, lane = row_facts(
        clusters_ref[...].reshape(1, clusters_ref.shape[0]), owner_ref, me_ref[0]
    )
    width = rows_ref.shape[1]
    total = 8 * packet_rows
    copies[2].wait()
    placed = jnp.dot(
        ones_at(total, packet * packet_rows + rank), rows_ref[...], preferred_element_type=f32
    )
    labels = jnp.where(hits(64, packet * 8 + part), (cluster + 1).astype(f32), 0.0).astype(bf16)
    ids = lax.dot_general(
        labels, ones_at(width, lane), (((1,), (1,)), ((), ())), preferred_element_type=f32
    ).astype(bf16)
    source = lax.broadcasted_iota(jnp.int32, (1, 64), 1)
    placed_ids = jnp.dot(
        ones_at(total, (source // 8) * packet_rows + filled + source % 8),
        ids,
        preferred_element_type=f32,
    )
    both = (placed + placed_ids).astype(bf16)
    for n in range(8):
        out_refs[n][...] = both[n * packet_rows : (n + 1) * packet_rows]


def spans(p):
    found = []
    for n in range(8):
        low = max(p * block_keys, n * filled) - n * filled
        high = min((p + 1) * block_keys, (n + 1) * filled) - n * filled
        if low < high:
            found.append((n, low, high))
    return found


def pack_kernel(*refs):
    packets = [ref[...].astype(f32) for ref in refs[:8]]
    big_ref, small_ref = refs[8:]
    blocks = [
        jnp.concatenate([packets[n][low:high] for n, low, high in spans(p)], axis=0)
        for p in range(parts)
    ]
    ids = sum(packet[filled:packet_rows] for packet in packets)
    at = lax.broadcasted_iota(jnp.int32, ids.shape, 0)
    big_ref[0 : 2 * block_keys, :] = jnp.concatenate(blocks[:2], axis=0).astype(bf16)
    big_ref[2 * block_keys : big_rows, :] = jnp.concatenate(
        [jnp.where(at < 2, ids, 0.0), jnp.zeros_like(ids)], axis=0
    ).astype(bf16)
    last = jnp.sum(jnp.where(at == 2, ids, 0.0), axis=0, keepdims=True)
    small_ref[...] = jnp.concatenate([blocks[2], jnp.where(at == 0, last, 0.0)], axis=0).astype(bf16)


def pack(packets):
    width = packets[0].shape[1]
    return pl.pallas_call(
        pack_kernel,
        out_shape=[jax.ShapeDtypeStruct((count, width), bf16) for count in (big_rows, small_rows)],
        in_specs=vmem_specs(8),
        out_specs=vmem_specs(2),
        compiler_params=params,
        name="pack",
    )(*packets)


def column_of(row):
    count = block_keys
    wide = row.shape[1]
    eye = lax.broadcasted_iota(jnp.int32, (count, wide), 0) == lax.broadcasted_iota(
        jnp.int32, (count, wide), 1
    )
    return jnp.sum(jnp.where(eye, row, 0.0), axis=1, keepdims=True)


def row_of(column, wide):
    count = column.shape[0]
    eye = lax.broadcasted_iota(jnp.int32, (count, wide), 0) == lax.broadcasted_iota(
        jnp.int32, (count, wide), 1
    )
    return jnp.sum(jnp.where(eye, column, 0.0), axis=0, keepdims=True)


def high_low(value):
    high = value.astype(bf16).astype(f32)
    return high, value - high


def gather_rows(refs, wides, store):
    id_rows = []
    for ref, wide in zip(refs, wides):
        step, count = (big_rows, 2) if wide else (small_rows, 1)
        for start in range(0, ref.shape[0], step):
            end = start + count * block_keys
            first = len(id_rows) * block_keys
            store[first : first + count * block_keys, :] = ref[start:end, :]
            ids = ref[end : end + 8 * count, 0:256].astype(f32)[0:8]
            id_rows += [ids, pltpu.roll(ids, 7, 0)][:count]
    return id_rows


def side_by_side(id_rows):
    pieces = []
    for even, odd in zip(id_rows[::2], id_rows[1::2]):
        odd = pltpu.roll(odd, 64, 1)
        pieces += [even[:, 0:128], even[:, 128:256] + odd[:, 0:128], odd[:, 128:256]]
    return jnp.concatenate(pieces, axis=1)[0:1]


def flash_kernel(wides, first, owns, finish, *refs):
    refs = list(refs)
    count = len(owns)
    q_refs = [[refs.pop(0), refs.pop(0)] for _ in range(count)]
    key_refs = [refs.pop(0) for _ in wides]
    states = None if first else [[refs.pop(0) for _ in range(3)] for _ in range(count)]
    outs = [[refs.pop(0)] if finish else [refs.pop(0) for _ in range(3)] for _ in range(count)]
    keys, queries, labels = refs
    width = q_refs[0][0].shape[1]
    scale = score_scale / math.sqrt(width) * log2e
    key_id = side_by_side(gather_rows(key_refs, wides, keys))
    other = jnp.where(key_id == 0.0, masked, -penalty * log2e)
    for n in range(count):
        wide_ids = q_refs[n][0][2 * block_keys : big_rows, 0:256].astype(f32)
        small_ids = q_refs[n][1][block_keys:small_rows, 0:256].astype(f32)
        for p, ids in enumerate((wide_ids[0:1], wide_ids[1:2], small_ids[0:1])):
            labels[n, p * block_keys : (p + 1) * block_keys, :] = column_of(ids)
    work = [(n, start, rows) for n in range(count) for start, rows in ((0, 384), (384, 192))]

    def product(n, start, query_rows):
        rows = q_refs[n][start // 384][0:query_rows, :]
        return lax.dot_general(
            rows, keys[...], (((1,), (1,)), ((), ())), preferred_element_type=f32
        )

    ahead = product(*work[0])
    for k, (n, start, query_rows) in enumerate(work):
        at = slice(start, start + query_rows)
        scores = ahead
        if k + 1 < len(work):
            ahead = product(*work[k + 1])
        scores = scores * scale + jnp.where(key_id == labels[n, at, :], 0.0, other)
        if first and owns[n]:
            row = lax.broadcasted_iota(jnp.int32, scores.shape, 0) + start
            scores = jnp.where(
                row == lax.broadcasted_iota(jnp.int32, scores.shape, 1), masked, scores
            )
        highest = jnp.max(scores, axis=1, keepdims=True)
        if first:
            peak = jnp.maximum(highest, 0.0)
        else:
            former = states[n][0][at, :]
            peak = jnp.maximum(former, highest)
            fade = jnp.exp2(former - peak)
        weights = jnp.exp2(scores - peak)
        mass = jnp.sum(weights, axis=1, keepdims=True)
        acc = jnp.dot(weights.astype(bf16), keys[...], preferred_element_type=f32)
        if not first:
            mass = mass + states[n][1][at, :] * fade
            acc = acc + states[n][2][at, :] * fade
        elif owns[n]:
            mass = mass + jnp.exp2(-peak)
        if not finish:
            outs[n][0][at, :], outs[n][1][at, :], outs[n][2][at, :] = peak, mass, acc
            continue
        safe = jnp.where(mass > 0.0, mass, 1.0)
        outs[n][0][at, :] = (acc / safe).astype(bf16)
        labels[n, at, :] = jnp.where(mass > 0.0, peak + jnp.log2(safe), masked)
    if finish:
        rows = parts * block_keys
        for n in range(count):
            here = lax.broadcasted_iota(jnp.int32, (16, width), 0)
            tails = jnp.zeros((16, width), f32)
            for p in range(parts):
                high, low = high_low(labels[n, p * block_keys : (p + 1) * block_keys, :])
                tails = tails + jnp.where(here == 2 * p, row_of(high, width), 0.0)
                tails = tails + jnp.where(here == 2 * p + 1, row_of(low, width), 0.0)
            outs[n][0][rows : rows + 16, :] = tails.astype(bf16)


def flash(qs, owns, key_arrays, states, finish):
    width = qs[0][0].shape[1]
    wides = [wide for _, wide in key_arrays]
    key_arrays = [a for a, _ in key_arrays]
    total = sum(
        a.shape[0] // big_rows * 2 if wide else a.shape[0] // small_rows
        for a, wide in zip(key_arrays, wides)
    )
    total *= block_keys
    rows = parts * block_keys
    first = states is None
    if finish:
        each = [jax.ShapeDtypeStruct((rows + 16, width), bf16)]
    else:
        each = [
            jax.ShapeDtypeStruct((rows, 1), f32),
            jax.ShapeDtypeStruct((rows, 1), f32),
            jax.ShapeDtypeStruct((rows, width), f32),
        ]
    count = len(qs)
    args = [a for q in qs for a in q] + key_arrays + ([] if first else [a for state in states for a in state])
    out = pl.pallas_call(
        functools.partial(flash_kernel, wides, first, owns, finish),
        out_shape=each * count,
        in_specs=vmem_specs(len(args)),
        out_specs=vmem_specs(len(each) * count),
        scratch_shapes=[
            pltpu.VMEM((total, width), bf16),
            pltpu.VMEM((8, 128), bf16),
            pltpu.VMEM((count, rows, 1), f32),
        ],
        compiler_params=params,
        cost_estimate=pl.CostEstimate(
            flops=8 * count * rows * total * width,
            transcendentals=count * rows * total,
            bytes_accessed=2 * total * width + 6 * count * rows * width,
        ),
        name="flash",
    )(*args)
    if finish:
        return out
    return [tuple(out[3 * n : 3 * n + 3]) for n in range(count)]


def combine_kernel(m_ref, l_ref, acc_ref, other_ref, *out_refs):
    width = acc_ref.shape[1]
    rows = parts * block_keys
    tails = other_ref[rows : rows + 16, :].astype(f32)
    mixes, levels = [], []
    here = lax.broadcasted_iota(jnp.int32, (8, width), 0)
    for p in range(parts):
        at = slice(p * block_keys, (p + 1) * block_keys)
        level = column_of(
            tails[2 * p : 2 * p + 1, 0:256] + tails[2 * p + 1 : 2 * p + 2, 0:256]
        )
        peak = jnp.maximum(m_ref[at, :], level)
        mine = jnp.exp2(m_ref[at, :] - peak)
        theirs = jnp.exp2(level - peak)
        total = l_ref[at, :] * mine + theirs
        mixes.append(
            (acc_ref[at, :] * mine + other_ref[at, :].astype(f32) * theirs) / total
        )
        high, low = high_low((peak + jnp.log2(total)) * ln2)
        tail = jnp.where(here == p, row_of(high, width), 0.0) + jnp.where(
            here == 3 + p, row_of(low, width), 0.0
        )
        levels = tail if p == 0 else levels + tail
    for n in range(8):
        pieces = [
            mixes[p][n * filled + low - p * block_keys : n * filled + high - p * block_keys]
            for p in range(parts)
            for other, low, high in spans(p)
            if other == n
        ]
        out_refs[n][...] = jnp.concatenate(pieces + [levels], axis=0).astype(bf16)


def final_kernel(me_ref, owner_ref, clusters_ref, *refs):
    backs, (rows_ref, mass_ref, back) = refs[:8], refs[8:]
    _, packet, rank, part, lane = row_facts(
        clusters_ref[...].reshape(1, clusters_ref.shape[0]), owner_ref, me_ref[0]
    )
    for n in range(8):
        back[n * packet_rows : (n + 1) * packet_rows, :] = backs[n][...]
    rows_ref[...] = lax.dot_general(
        ones_at(8 * packet_rows, packet * packet_rows + rank),
        back[...],
        (((0,), (0,)), ((), ())),
        preferred_element_type=f32,
    ).astype(bf16)
    levels = jnp.concatenate(
        [backs[n][64:packet_rows, 0:256].astype(f32)[8:16] for n in range(8)], axis=0
    ).astype(bf16)
    found = jnp.dot(levels, ones_at(256, lane), preferred_element_type=f32)
    chosen = hits(64, packet * 8 + part) | hits(64, packet * 8 + 3 + part)
    mass_ref[...] = jnp.sum(jnp.where(chosen, found, 0.0), axis=0, keepdims=True).reshape(
        mass_ref.shape
    )


def links(mesh):
    side = 4

    def number(y, c, x, z):
        return ((y * 2 + c) * side + x) * side + z

    places = [
        (y, c, x, z) for y in range(side) for c in range(2) for x in range(side) for z in range(side)
    ]

    def pairs(move):
        return [(number(*at), number(*move(*at))) for at in places]

    dims = [
        pairs(lambda y, c, x, z: (y, c, x ^ 3, z)),
        pairs(lambda y, c, x, z: (y ^ 3, c, x, z)),
        pairs(lambda y, c, x, z: (y, c, x, z ^ 3)),
    ]
    swap = pairs(lambda y, c, x, z: (y, c ^ 1, x, z))
    trips = [
        pairs(lambda y, c, x, z, m=m: (y ^ (m >> 1 & 1), c, x ^ (m & 1), z ^ (m >> 2)))
        for m in (0, 1, 2, 4, 3, 5, 6, 7)
    ]
    return dims, swap, trips


def per_device(dims, swap, trips, embeddings, clusters, cluster_owner):
    rows, width = embeddings.shape
    send = lambda a, pairs: lax.ppermute(a, axes, pairs)
    group_axis, tile = lax.axis_index("group"), lax.axis_index("tile")
    kind = lambda at: (at + 1) // 2 % 2
    me = kind(tile // 4) + 2 * kind(group_axis // 2) + 4 * kind(tile % 4)
    me = me.astype(jnp.int32).reshape(1)
    smem = pl.BlockSpec(memory_space=pltpu.SMEM)
    packet = jax.ShapeDtypeStruct((packet_rows, width), bf16)
    packets = pl.pallas_call(
        place_kernel,
        out_shape=[packet] * 8,
        in_specs=[smem] + [pl.BlockSpec(memory_space=pltpu.HBM)] * 3,
        out_specs=vmem_specs(8),
        scratch_shapes=[
            pltpu.SMEM(cluster_owner.shape, jnp.int32),
            pltpu.VMEM(clusters.shape, jnp.int32),
            pltpu.VMEM(embeddings.shape, bf16),
            pltpu.SemaphoreType.DMA((3,)),
        ],
        compiler_params=params,
        name="place",
    )(
        me,
        *(pltpu.with_memory_space_constraint(a, pltpu.HBM) for a in (cluster_owner, clusters, embeddings)),
    )
    arrived = [packets[0]] + [send(packets[n], trips[n]) for n in range(1, 8)]
    big, small = pack(arrived)
    wide = [
        [pair for pair in dims[s % 3] if pair[0] // 16 % 2 == 0]
        + [pair for pair in dims[(s + 1) % 3] if pair[0] // 16 % 2 == 1]
        for s in range(3)
    ]
    narrow = [dims[(s + 2) % 3] for s in range(3)]
    big0, small0 = send(big, wide[0]), send(small, narrow[0])
    q_own, q_other = (big, small), (send(big, swap), send(small, swap))
    big0, small0 = lax.optimization_barrier((big0, small0))
    big, small = jnp.concatenate([big, big0], axis=0), jnp.concatenate([small, small0], axis=0)
    big1, small1 = send(big, wide[1]), send(small, narrow[1])
    queries, owns = [q_other, q_own], [False, True]
    pairs = lambda *units: list(zip(units, (True, False) * 2))
    begin = pairs(*q_own, big0, small0)
    states = flash(queries[1:], owns[1:], begin, None, False)
    big, small, states[0] = lax.optimization_barrier((big, small, states[0]))
    states = flash(queries[:1], owns[:1], begin, None, False) + states
    big2, small2 = send(big, wide[2]), send(small, narrow[2])
    big3, small3 = send(big1, wide[2]), send(small1, narrow[2])
    states = flash(queries, owns, pairs(big1, small1), states, False)
    states = flash(queries, owns, pairs(big2, small2), states, False)
    (partial,) = flash(queries[:1], owns[:1], pairs(big3, small3), states[:1], True)
    (mine,) = flash(queries[1:], owns[1:], pairs(big3, small3), states[1:], False)
    theirs = send(partial, swap)
    answers = pl.pallas_call(
        combine_kernel,
        out_shape=[packet] * 8,
        in_specs=vmem_specs(4),
        out_specs=vmem_specs(8),
        compiler_params=params,
        name="combine",
    )(*mine, theirs)
    back = [answers[0]] + [send(answers[n], trips[n]) for n in range(1, 8)]
    neighbours, log_mass = pl.pallas_call(
        final_kernel,
        out_shape=[jax.ShapeDtypeStruct((rows, width), bf16), jax.ShapeDtypeStruct((rows,), f32)],
        in_specs=[smem, smem] + vmem_specs(9),
        out_specs=vmem_specs(2),
        scratch_shapes=[pltpu.VMEM((8 * packet_rows, width), bf16)],
        compiler_params=params,
        name="final",
    )(me, cluster_owner, clusters, *back)
    return neighbours, log_mass


def solution(mesh):
    placed = (P(axes, None), P(axes), P())
    dims, swap, trips = links(mesh)
    return jax.shard_map(
        functools.partial(per_device, dims, swap, trips),
        mesh=mesh,
        in_specs=placed,
        out_specs=(P(axes, None), P(axes)),
        check_vma=False,
    )
```

```python
import functools
import math

import jax
import jax.numpy as jnp
from jax import lax
from jax.experimental import pallas as pl
from jax.experimental.pallas import tpu as pltpu
from jax.sharding import PartitionSpec as P

score_scale = 3.0
penalty = 2.0
log2e = math.log2(math.e)
ln2 = math.log(2.0)
masked = -1e30
axes = ("group", "tile")
parts = 3
filled = 72
packet_rows = 80
block_keys = 192
big_rows = 400
small_rows = 200
query_rows = 288
f32 = jnp.float32
bf16 = jnp.bfloat16


def vmem_specs(count):
    return [pl.BlockSpec(memory_space=pltpu.VMEM) for _ in range(count)]


params = pltpu.CompilerParams(vmem_limit_bytes=32 * 1024 * 1024)


def row_facts(cluster, owner_ref, me):
    rows = cluster.shape[1]
    group = jnp.zeros_like(cluster)
    for number in range(owner_ref.shape[0]):
        group = jnp.where(cluster == number, owner_ref[number], group)
    member = lax.broadcasted_iota(jnp.int32, (8, rows), 0) == group
    upper = lax.broadcasted_iota(jnp.int32, (rows, rows), 0) < lax.broadcasted_iota(
        jnp.int32, (rows, rows), 1
    )
    counts = jnp.dot(
        member.astype(f32).astype(bf16), upper.astype(f32).astype(bf16), preferred_element_type=f32
    )
    rank = jnp.sum(jnp.where(member, counts, 0.0), axis=0, keepdims=True).astype(jnp.int32)
    change = group ^ me
    packet = jnp.where(change == 3, 4, jnp.where(change == 4, 3, change))
    slot = packet * filled + rank
    part = (slot >= block_keys).astype(jnp.int32) + (slot >= 2 * block_keys).astype(jnp.int32)
    return cluster, packet, rank, part, slot - part * block_keys


def hits(count, target):
    shape = (count, target.shape[1])
    return lax.broadcasted_iota(jnp.int32, shape, 0) == target


def ones_at(count, target):
    return hits(count, target).astype(f32).astype(bf16)


def place_kernel(me_ref, owner_hbm, clusters_hbm, rows_hbm, *refs):
    out_refs, (owner_ref, clusters_ref, rows_ref, done) = refs[:8], refs[8:]
    copies = [
        pltpu.make_async_copy(source, target, done.at[n])
        for n, (source, target) in enumerate(
            ((owner_hbm, owner_ref), (clusters_hbm, clusters_ref), (rows_hbm, rows_ref))
        )
    ]
    for copy in copies:
        copy.start()
    copies[0].wait()
    copies[1].wait()
    cluster, packet, rank, part, lane = row_facts(
        clusters_ref[...].reshape(1, clusters_ref.shape[0]), owner_ref, me_ref[0]
    )
    width = rows_ref.shape[1]
    total = 8 * packet_rows
    copies[2].wait()
    placed = jnp.dot(
        ones_at(total, packet * packet_rows + rank), rows_ref[...], preferred_element_type=f32
    )
    labels = jnp.where(hits(64, packet * 8 + part), (cluster + 1).astype(f32), 0.0).astype(bf16)
    ids = lax.dot_general(
        labels, ones_at(width, lane), (((1,), (1,)), ((), ())), preferred_element_type=f32
    ).astype(bf16)
    source = lax.broadcasted_iota(jnp.int32, (1, 64), 1)
    placed_ids = jnp.dot(
        ones_at(total, (source // 8) * packet_rows + filled + source % 8),
        ids,
        preferred_element_type=f32,
    )
    both = (placed + placed_ids).astype(bf16)
    for n in range(8):
        out_refs[n][...] = both[n * packet_rows : (n + 1) * packet_rows]


def spans(p):
    found = []
    for n in range(8):
        low = max(p * block_keys, n * filled) - n * filled
        high = min((p + 1) * block_keys, (n + 1) * filled) - n * filled
        if low < high:
            found.append((n, low, high))
    return found


def pack_kernel(blocks, names, *refs):
    packets = {n: ref[...].astype(f32) for n, ref in zip(names, refs)}
    ids = sum(packet[filled:packet_rows] for packet in packets.values())
    at = lax.broadcasted_iota(jnp.int32, ids.shape, 0)
    rows = [packets[n][low:high] for p in blocks for n, low, high in spans(p)]
    if len(blocks) == 2:
        tail = [jnp.where(at < 2, ids, 0.0), jnp.zeros_like(ids)]
    else:
        last = jnp.sum(jnp.where(at == 2, ids, 0.0), axis=0, keepdims=True)
        tail = [jnp.where(at == 0, last, 0.0)]
    refs[-1][...] = jnp.concatenate(rows + tail, axis=0).astype(bf16)


def pack(blocks, packets):
    names = sorted({n for p in blocks for n, _, _ in spans(p)})
    rows, width = (big_rows if len(blocks) == 2 else small_rows), packets[0].shape[1]
    return pl.pallas_call(
        functools.partial(pack_kernel, blocks, names),
        out_shape=jax.ShapeDtypeStruct((rows, width), bf16),
        in_specs=vmem_specs(len(names)),
        out_specs=vmem_specs(1)[0],
        compiler_params=params,
        name="pack",
    )(*[packets[n] for n in names])


def column_of(row, count=block_keys):
    wide = row.shape[1]
    eye = lax.broadcasted_iota(jnp.int32, (count, wide), 0) == lax.broadcasted_iota(
        jnp.int32, (count, wide), 1
    )
    return jnp.sum(jnp.where(eye, row, 0.0), axis=1, keepdims=True)


def row_of(column, wide):
    count = column.shape[0]
    eye = lax.broadcasted_iota(jnp.int32, (count, wide), 0) == lax.broadcasted_iota(
        jnp.int32, (count, wide), 1
    )
    return jnp.sum(jnp.where(eye, column, 0.0), axis=0, keepdims=True)


def high_low(value):
    high = value.astype(bf16).astype(f32)
    return high, value - high


def gather_rows(refs, wides, store):
    id_rows = []
    for ref, wide in zip(refs, wides):
        step, count = (big_rows, 2) if wide else (small_rows, 1)
        for start in range(0, ref.shape[0], step):
            end = start + count * block_keys
            first = len(id_rows) * block_keys
            store[first : first + count * block_keys, :] = ref[start:end, :]
            ids = ref[end : end + 8 * count, 0:256].astype(f32)[0:8]
            id_rows += [ids, pltpu.roll(ids, 7, 0)][:count]
    return id_rows


def side_by_side(id_rows):
    pieces = []
    for even, odd in zip(id_rows[::2], id_rows[1::2]):
        odd = pltpu.roll(odd, 64, 1)
        pieces += [even[:, 0:128], even[:, 128:256] + odd[:, 0:128], odd[:, 128:256]]
    return jnp.concatenate(pieces, axis=1)[0:1]


def flash_kernel(wides, first, owns, finish, *refs):
    refs = list(refs)
    count = len(owns)
    q_refs = [[refs.pop(0), refs.pop(0)] for _ in range(count)]
    key_refs = [refs.pop(0) for _ in wides]
    states = None if first else [[refs.pop(0) for _ in range(3)] for _ in range(count)]
    outs = [[refs.pop(0)] if finish else [refs.pop(0) for _ in range(3)] for _ in range(count)]
    keys, queries, labels = refs
    width = q_refs[0][0].shape[1]
    scale = score_scale / math.sqrt(width) * log2e
    key_id = side_by_side(gather_rows(key_refs, wides, keys))
    other = jnp.where(key_id == 0.0, masked, -penalty * log2e)
    for n in range(count):
        wide_ids = q_refs[n][0][2 * block_keys : big_rows, 0:256].astype(f32)
        small_ids = q_refs[n][1][block_keys:small_rows, 0:256].astype(f32)
        for p, ids in enumerate((wide_ids[0:1], wide_ids[1:2], small_ids[0:1])):
            labels[n, p * block_keys : (p + 1) * block_keys, :] = column_of(ids)
    work = [(n, start, rows) for n in range(count) for start, rows in ((0, 384), (384, 192))]

    def product(n, start, query_rows):
        rows = q_refs[n][start // 384][0:query_rows, :]
        return lax.dot_general(
            rows, keys[...], (((1,), (1,)), ((), ())), preferred_element_type=f32
        )

    ahead = product(*work[0])
    for k, (n, start, query_rows) in enumerate(work):
        at = slice(start, start + query_rows)
        scores = ahead
        if k + 1 < len(work):
            ahead = product(*work[k + 1])
        scores = scores * scale + jnp.where(key_id == labels[n, at, :], 0.0, other)
        if first and owns[n]:
            row = lax.broadcasted_iota(jnp.int32, scores.shape, 0) + start
            scores = jnp.where(
                row == lax.broadcasted_iota(jnp.int32, scores.shape, 1), masked, scores
            )
        highest = jnp.max(scores, axis=1, keepdims=True)
        if first:
            peak = jnp.maximum(highest, 0.0)
        else:
            former = states[n][0][at, :]
            peak = jnp.maximum(former, highest)
            fade = jnp.exp2(former - peak)
        weights = jnp.exp2(scores - peak)
        mass = jnp.sum(weights, axis=1, keepdims=True)
        acc = jnp.dot(weights.astype(bf16), keys[...], preferred_element_type=f32)
        if not first:
            mass = mass + states[n][1][at, :] * fade
            acc = acc + states[n][2][at, :] * fade
        elif owns[n]:
            mass = mass + jnp.exp2(-peak)
        if not finish:
            outs[n][0][at, :], outs[n][1][at, :], outs[n][2][at, :] = peak, mass, acc
            continue
        safe = jnp.where(mass > 0.0, mass, 1.0)
        outs[n][0][at, :] = (acc / safe).astype(bf16)
        labels[n, at, :] = jnp.where(mass > 0.0, peak + jnp.log2(safe), masked)
    if finish:
        rows = parts * block_keys
        for n in range(count):
            here = lax.broadcasted_iota(jnp.int32, (16, width), 0)
            tails = jnp.zeros((16, width), f32)
            for p in range(parts):
                high, low = high_low(labels[n, p * block_keys : (p + 1) * block_keys, :])
                tails = tails + jnp.where(here == 2 * p, row_of(high, width), 0.0)
                tails = tails + jnp.where(here == 2 * p + 1, row_of(low, width), 0.0)
            outs[n][0][rows : rows + 16, :] = tails.astype(bf16)


def flash(qs, owns, key_arrays, states, finish):
    width = qs[0][0].shape[1]
    wides = [wide for _, wide in key_arrays]
    key_arrays = [a for a, _ in key_arrays]
    total = sum(
        a.shape[0] // big_rows * 2 if wide else a.shape[0] // small_rows
        for a, wide in zip(key_arrays, wides)
    )
    total *= block_keys
    rows = parts * block_keys
    first = states is None
    if finish:
        each = [jax.ShapeDtypeStruct((rows + 16, width), bf16)]
    else:
        each = [
            jax.ShapeDtypeStruct((rows, 1), f32),
            jax.ShapeDtypeStruct((rows, 1), f32),
            jax.ShapeDtypeStruct((rows, width), f32),
        ]
    count = len(qs)
    args = [a for q in qs for a in q] + key_arrays + ([] if first else [a for state in states for a in state])
    out = pl.pallas_call(
        functools.partial(flash_kernel, wides, first, owns, finish),
        out_shape=each * count,
        in_specs=vmem_specs(len(args)),
        out_specs=vmem_specs(len(each) * count),
        scratch_shapes=[
            pltpu.VMEM((total, width), bf16),
            pltpu.VMEM((8, 128), bf16),
            pltpu.VMEM((count, rows, 1), f32),
        ],
        compiler_params=params,
        cost_estimate=pl.CostEstimate(
            flops=8 * count * rows * total * width,
            transcendentals=count * rows * total,
            bytes_accessed=2 * total * width + 6 * count * rows * width,
        ),
        name="flash",
    )(*args)
    if finish:
        return out
    return [tuple(out[3 * n : 3 * n + 3]) for n in range(count)]


def combine_kernel(m_ref, l_ref, acc_ref, other_ref, *out_refs):
    width = acc_ref.shape[1]
    rows = parts * block_keys
    tails = other_ref[rows : rows + 16, :].astype(f32)
    mixes, levels = [], []
    here = lax.broadcasted_iota(jnp.int32, (8, width), 0)
    for p in range(parts):
        at = slice(p * block_keys, (p + 1) * block_keys)
        level = column_of(
            tails[2 * p : 2 * p + 1, 0:256] + tails[2 * p + 1 : 2 * p + 2, 0:256]
        )
        peak = jnp.maximum(m_ref[at, :], level)
        mine = jnp.exp2(m_ref[at, :] - peak)
        theirs = jnp.exp2(level - peak)
        total = l_ref[at, :] * mine + theirs
        mixes.append(
            (acc_ref[at, :] * mine + other_ref[at, :].astype(f32) * theirs) / total
        )
        high, low = high_low((peak + jnp.log2(total)) * ln2)
        tail = jnp.where(here == p, row_of(high, width), 0.0) + jnp.where(
            here == 3 + p, row_of(low, width), 0.0
        )
        levels = tail if p == 0 else levels + tail
    for n in range(8):
        pieces = [
            mixes[p][n * filled + low - p * block_keys : n * filled + high - p * block_keys]
            for p in range(parts)
            for other, low, high in spans(p)
            if other == n
        ]
        out_refs[n][...] = jnp.concatenate(pieces + [levels], axis=0).astype(bf16)


def choose_kernel(me_ref, owner_ref, clusters_ref, rows_ref, lanes_ref, chosen_ref):
    _, packet, rank, part, lane = row_facts(
        clusters_ref[...].reshape(1, clusters_ref.shape[0]), owner_ref, me_ref[0]
    )
    count, total = rows_ref.shape
    target = column_of((packet * packet_rows + rank).astype(f32), count).astype(jnp.int32)
    at = lax.broadcasted_iota(jnp.int32, (count, total), 1)
    rows_ref[...] = (at == target).astype(f32).astype(bf16)
    lanes_ref[...] = ones_at(lanes_ref.shape[0], lane)
    chosen = hits(64, packet * 8 + part) | hits(64, packet * 8 + 3 + part)
    chosen_ref[...] = chosen.astype(f32)


def final_kernel(choice_ref, lanes_ref, chosen_ref, *refs):
    backs, (rows_ref, mass_ref, back) = refs[:8], refs[8:]
    for n in range(8):
        back[n * packet_rows : (n + 1) * packet_rows, :] = backs[n][...]
    rows_ref[...] = jnp.dot(
        choice_ref[...], back[...], preferred_element_type=f32
    ).astype(bf16)
    levels = jnp.concatenate(
        [backs[n][64:packet_rows, 0:256].astype(f32)[8:16] for n in range(8)], axis=0
    ).astype(bf16)
    found = jnp.dot(levels, lanes_ref[...], preferred_element_type=f32)
    mass_ref[...] = jnp.sum(
        jnp.where(chosen_ref[...] > 0.0, found, 0.0), axis=0, keepdims=True
    ).reshape(mass_ref.shape)


def links(mesh):
    side = 4

    def number(y, c, x, z):
        return ((y * 2 + c) * side + x) * side + z

    places = [
        (y, c, x, z) for y in range(side) for c in range(2) for x in range(side) for z in range(side)
    ]

    def pairs(move):
        return [(number(*at), number(*move(*at))) for at in places]

    dims = [
        pairs(lambda y, c, x, z: (y, c, x ^ 3, z)),
        pairs(lambda y, c, x, z: (y ^ 3, c, x, z)),
        pairs(lambda y, c, x, z: (y, c, x, z ^ 3)),
    ]
    swap = pairs(lambda y, c, x, z: (y, c ^ 1, x, z))
    trips = [
        pairs(lambda y, c, x, z, m=m: (y ^ (m >> 1 & 1), c, x ^ (m & 1), z ^ (m >> 2)))
        for m in (0, 1, 2, 4, 3, 5, 6, 7)
    ]
    return dims, swap, trips


def per_device(dims, swap, trips, embeddings, clusters, cluster_owner):
    rows, width = embeddings.shape
    send = lambda a, pairs: lax.ppermute(a, axes, pairs)
    group_axis, tile = lax.axis_index("group"), lax.axis_index("tile")
    kind = lambda at: (at + 1) // 2 % 2
    me = kind(tile // 4) + 2 * kind(group_axis // 2) + 4 * kind(tile % 4)
    me = me.astype(jnp.int32).reshape(1)
    smem = pl.BlockSpec(memory_space=pltpu.SMEM)
    packet = jax.ShapeDtypeStruct((packet_rows, width), bf16)
    packets = pl.pallas_call(
        place_kernel,
        out_shape=[packet] * 8,
        in_specs=[smem] + [pl.BlockSpec(memory_space=pltpu.HBM)] * 3,
        out_specs=vmem_specs(8),
        scratch_shapes=[
            pltpu.SMEM(cluster_owner.shape, jnp.int32),
            pltpu.VMEM(clusters.shape, jnp.int32),
            pltpu.VMEM(embeddings.shape, bf16),
            pltpu.SemaphoreType.DMA((3,)),
        ],
        compiler_params=params,
        name="place",
    )(
        me,
        *(pltpu.with_memory_space_constraint(a, pltpu.HBM) for a in (cluster_owner, clusters, embeddings)),
    )
    arrived = [packets[0]] + [send(packets[n], trips[n]) for n in range(1, 8)]
    big, small = pack((0, 1), arrived), pack((2,), arrived)
    wide = [
        [pair for pair in dims[s % 3] if pair[0] // 16 % 2 == 0]
        + [pair for pair in dims[(s + 1) % 3] if pair[0] // 16 % 2 == 1]
        for s in range(3)
    ]
    narrow = [dims[(s + 2) % 3] for s in range(3)]
    big0, small0 = send(big, wide[0]), send(small, narrow[0])
    q_own, q_other = (big, small), (send(big, swap), send(small, swap))
    big, small = jnp.concatenate([big, big0], axis=0), jnp.concatenate([small, small0], axis=0)
    big1, small1 = send(big, wide[1]), send(small, narrow[1])
    queries, owns = [q_other, q_own], [False, True]
    pairs = lambda *units: list(zip(units, (True, False) * 2))
    begin = pairs(*q_own, big0, small0)
    states = flash(queries[1:], owns[1:], begin, None, False)
    big, small, states[0] = lax.optimization_barrier((big, small, states[0]))
    states = flash(queries[:1], owns[:1], begin, None, False) + states
    big2, small2 = send(big, wide[2]), send(small, narrow[2])
    big3, small3 = send(big1, wide[2]), send(small1, narrow[2])
    states = flash(queries, owns, pairs(big1, small1), states, False)
    states = flash(queries, owns, pairs(big2, small2), states, False)
    (partial,) = flash(queries[:1], owns[:1], pairs(big3, small3), states[:1], True)
    (mine,) = flash(queries[1:], owns[1:], pairs(big3, small3), states[1:], False)
    theirs = send(partial, swap)
    answers = pl.pallas_call(
        combine_kernel,
        out_shape=[packet] * 8,
        in_specs=vmem_specs(4),
        out_specs=vmem_specs(8),
        compiler_params=params,
        name="combine",
    )(*mine, theirs)
    back = [answers[0]] + [send(answers[n], trips[n]) for n in range(1, 8)]
    choice = pl.pallas_call(
        choose_kernel,
        out_shape=[
            jax.ShapeDtypeStruct((rows, 8 * packet_rows), bf16),
            jax.ShapeDtypeStruct((256, rows), bf16),
            jax.ShapeDtypeStruct((64, rows), f32),
        ],
        in_specs=[smem, smem] + vmem_specs(1),
        out_specs=vmem_specs(3),
        compiler_params=params,
        name="choose",
    )(me, cluster_owner, clusters)
    neighbours, log_mass = pl.pallas_call(
        final_kernel,
        out_shape=[jax.ShapeDtypeStruct((rows, width), bf16), jax.ShapeDtypeStruct((rows,), f32)],
        in_specs=vmem_specs(11),
        out_specs=vmem_specs(2),
        scratch_shapes=[pltpu.VMEM((8 * packet_rows, width), bf16)],
        compiler_params=params,
        name="final",
    )(*choice, *back)
    return neighbours, log_mass


def solution(mesh):
    placed = (P(axes, None), P(axes), P())
    dims, swap, trips = links(mesh)
    return jax.shard_map(
        functools.partial(per_device, dims, swap, trips),
        mesh=mesh,
        in_specs=placed,
        out_specs=(P(axes, None), P(axes)),
        check_vma=False,
    )
```

```python
import functools
import math

import jax
import jax.numpy as jnp
from jax import lax
from jax.experimental import pallas as pl
from jax.experimental.pallas import tpu as pltpu
from jax.sharding import PartitionSpec as P

score_scale = 3.0
penalty = 2.0
log2e = math.log2(math.e)
ln2 = math.log(2.0)
masked = -1e30
axes = ("group", "tile")
parts = 3
filled = 72
packet_rows = 80
block_keys = 192
big_rows = 400
small_rows = 200
query_rows = 288
f32 = jnp.float32
bf16 = jnp.bfloat16


def vmem_specs(count):
    return [pl.BlockSpec(memory_space=pltpu.VMEM) for _ in range(count)]


params = pltpu.CompilerParams(vmem_limit_bytes=32 * 1024 * 1024)


def row_facts(cluster, owner_ref, me):
    rows = cluster.shape[1]
    group = jnp.zeros_like(cluster)
    for number in range(owner_ref.shape[0]):
        group = jnp.where(cluster == number, owner_ref[number], group)
    member = lax.broadcasted_iota(jnp.int32, (8, rows), 0) == group
    upper = lax.broadcasted_iota(jnp.int32, (rows, rows), 0) < lax.broadcasted_iota(
        jnp.int32, (rows, rows), 1
    )
    counts = jnp.dot(
        member.astype(f32).astype(bf16), upper.astype(f32).astype(bf16), preferred_element_type=f32
    )
    rank = jnp.sum(jnp.where(member, counts, 0.0), axis=0, keepdims=True).astype(jnp.int32)
    change = group ^ me
    packet = jnp.where(change == 3, 4, jnp.where(change == 4, 3, change))
    slot = packet * filled + rank
    part = (slot >= block_keys).astype(jnp.int32) + (slot >= 2 * block_keys).astype(jnp.int32)
    return cluster, packet, rank, part, slot - part * block_keys


def hits(count, target):
    shape = (count, target.shape[1])
    return lax.broadcasted_iota(jnp.int32, shape, 0) == target


def ones_at(count, target):
    return hits(count, target).astype(f32).astype(bf16)


def place_kernel(me_ref, owner_hbm, clusters_hbm, rows_hbm, *refs):
    out_refs, (owner_ref, clusters_ref, rows_ref, done) = refs[:8], refs[8:]
    copies = [
        pltpu.make_async_copy(source, target, done.at[n])
        for n, (source, target) in enumerate(
            ((owner_hbm, owner_ref), (clusters_hbm, clusters_ref), (rows_hbm, rows_ref))
        )
    ]
    for copy in copies:
        copy.start()
    copies[0].wait()
    copies[1].wait()
    cluster, packet, rank, part, lane = row_facts(
        clusters_ref[...].reshape(1, clusters_ref.shape[0]), owner_ref, me_ref[0]
    )
    width = rows_ref.shape[1]
    total = 8 * packet_rows
    copies[2].wait()
    placed = jnp.dot(
        ones_at(total, packet * packet_rows + rank), rows_ref[...], preferred_element_type=f32
    )
    labels = jnp.where(hits(64, packet * 8 + part), (cluster + 1).astype(f32), 0.0).astype(bf16)
    ids = lax.dot_general(
        labels, ones_at(width, lane), (((1,), (1,)), ((), ())), preferred_element_type=f32
    ).astype(bf16)
    source = lax.broadcasted_iota(jnp.int32, (1, 64), 1)
    placed_ids = jnp.dot(
        ones_at(total, (source // 8) * packet_rows + filled + source % 8),
        ids,
        preferred_element_type=f32,
    )
    both = (placed + placed_ids).astype(bf16)
    for n in range(8):
        out_refs[n][...] = both[n * packet_rows : (n + 1) * packet_rows]


def spans(p):
    found = []
    for n in range(8):
        low = max(p * block_keys, n * filled) - n * filled
        high = min((p + 1) * block_keys, (n + 1) * filled) - n * filled
        if low < high:
            found.append((n, low, high))
    return found


def pack_kernel(blocks, names, *refs):
    packets = {n: ref[...].astype(f32) for n, ref in zip(names, refs)}
    ids = sum(packet[filled:packet_rows] for packet in packets.values())
    at = lax.broadcasted_iota(jnp.int32, ids.shape, 0)
    rows = [packets[n][low:high] for p in blocks for n, low, high in spans(p)]
    if len(blocks) == 2:
        tail = [jnp.where(at < 2, ids, 0.0), jnp.zeros_like(ids)]
    else:
        last = jnp.sum(jnp.where(at == 2, ids, 0.0), axis=0, keepdims=True)
        tail = [jnp.where(at == 0, last, 0.0)]
    refs[-1][...] = jnp.concatenate(rows + tail, axis=0).astype(bf16)


def pack(blocks, packets):
    names = sorted({n for p in blocks for n, _, _ in spans(p)})
    rows, width = (big_rows if len(blocks) == 2 else small_rows), packets[0].shape[1]
    return pl.pallas_call(
        functools.partial(pack_kernel, blocks, names),
        out_shape=jax.ShapeDtypeStruct((rows, width), bf16),
        in_specs=vmem_specs(len(names)),
        out_specs=vmem_specs(1)[0],
        compiler_params=params,
        name="pack",
    )(*[packets[n] for n in names])


def column_of(row, count=block_keys):
    wide = row.shape[1]
    eye = lax.broadcasted_iota(jnp.int32, (count, wide), 0) == lax.broadcasted_iota(
        jnp.int32, (count, wide), 1
    )
    return jnp.sum(jnp.where(eye, row, 0.0), axis=1, keepdims=True)


def row_of(column, wide):
    count = column.shape[0]
    eye = lax.broadcasted_iota(jnp.int32, (count, wide), 0) == lax.broadcasted_iota(
        jnp.int32, (count, wide), 1
    )
    return jnp.sum(jnp.where(eye, column, 0.0), axis=0, keepdims=True)


def high_low(value):
    high = value.astype(bf16).astype(f32)
    return high, value - high


def gather_rows(refs, wides, store):
    id_rows = []
    for ref, wide in zip(refs, wides):
        step, count = (big_rows, 2) if wide else (small_rows, 1)
        for start in range(0, ref.shape[0], step):
            end = start + count * block_keys
            first = len(id_rows) * block_keys
            if store is not None:
                store[first : first + count * block_keys, :] = ref[start:end, :]
            ids = ref[end : end + 8 * count, 0:256].astype(f32)[0:8]
            id_rows += [ids, pltpu.roll(ids, 7, 0)][:count]
    return id_rows


def side_by_side(id_rows):
    pieces = []
    for even, odd in zip(id_rows[::2], id_rows[1::2]):
        odd = pltpu.roll(odd, 64, 1)
        pieces += [even[:, 0:128], even[:, 128:256] + odd[:, 0:128], odd[:, 128:256]]
    return jnp.concatenate(pieces, axis=1)[0:1]


def flash_kernel(wides, first, owns, finish, given, *refs):
    refs = list(refs)
    count = len(owns)
    q_refs = [[refs.pop(0), refs.pop(0)] for _ in range(count)]
    key_refs = [refs.pop(0) for _ in wides]
    keys = refs.pop(0) if given else None
    states = None if first else [[refs.pop(0) for _ in range(3)] for _ in range(count)]
    outs = [[refs.pop(0)] if finish else [refs.pop(0) for _ in range(3)] for _ in range(count)]
    if not given:
        keys = refs.pop(0)
    queries, labels = refs
    width = q_refs[0][0].shape[1]
    scale = score_scale / math.sqrt(width) * log2e
    key_id = side_by_side(gather_rows(key_refs, wides, None if given else keys))
    other = jnp.where(key_id == 0.0, masked, -penalty * log2e)
    for n in range(count):
        wide_ids = q_refs[n][0][2 * block_keys : big_rows, 0:256].astype(f32)
        small_ids = q_refs[n][1][block_keys:small_rows, 0:256].astype(f32)
        for p, ids in enumerate((wide_ids[0:1], wide_ids[1:2], small_ids[0:1])):
            labels[n, p * block_keys : (p + 1) * block_keys, :] = column_of(ids)
    work = [(n, start, rows) for n in range(count) for start, rows in ((0, 384), (384, 192))]

    def product(n, start, query_rows):
        rows = q_refs[n][start // 384][0:query_rows, :]
        return lax.dot_general(
            rows, keys[...], (((1,), (1,)), ((), ())), preferred_element_type=f32
        )

    ahead = product(*work[0])
    for k, (n, start, query_rows) in enumerate(work):
        at = slice(start, start + query_rows)
        scores = ahead
        if k + 1 < len(work):
            ahead = product(*work[k + 1])
        scores = scores * scale + jnp.where(key_id == labels[n, at, :], 0.0, other)
        if first and owns[n]:
            row = lax.broadcasted_iota(jnp.int32, scores.shape, 0) + start
            scores = jnp.where(
                row == lax.broadcasted_iota(jnp.int32, scores.shape, 1), masked, scores
            )
        highest = jnp.max(scores, axis=1, keepdims=True)
        if first:
            peak = jnp.maximum(highest, 0.0)
        else:
            former = states[n][0][at, :]
            peak = jnp.maximum(former, highest)
            fade = jnp.exp2(former - peak)
        weights = jnp.exp2(scores - peak)
        mass = jnp.sum(weights, axis=1, keepdims=True)
        acc = jnp.dot(weights.astype(bf16), keys[...], preferred_element_type=f32)
        if not first:
            mass = mass + states[n][1][at, :] * fade
            acc = acc + states[n][2][at, :] * fade
        elif owns[n]:
            mass = mass + jnp.exp2(-peak)
        if not finish:
            outs[n][0][at, :], outs[n][1][at, :], outs[n][2][at, :] = peak, mass, acc
            continue
        safe = jnp.where(mass > 0.0, mass, 1.0)
        outs[n][0][at, :] = (acc / safe).astype(bf16)
        labels[n, at, :] = jnp.where(mass > 0.0, peak + jnp.log2(safe), masked)
    if finish:
        rows = parts * block_keys
        for n in range(count):
            here = lax.broadcasted_iota(jnp.int32, (16, width), 0)
            tails = jnp.zeros((16, width), f32)
            for p in range(parts):
                high, low = high_low(labels[n, p * block_keys : (p + 1) * block_keys, :])
                tails = tails + jnp.where(here == 2 * p, row_of(high, width), 0.0)
                tails = tails + jnp.where(here == 2 * p + 1, row_of(low, width), 0.0)
            outs[n][0][rows : rows + 16, :] = tails.astype(bf16)


def flash(qs, owns, key_arrays, states, finish, gathered=None):
    width = qs[0][0].shape[1]
    wides = [wide for _, wide in key_arrays]
    key_arrays = [a for a, _ in key_arrays]
    total = sum(
        a.shape[0] // big_rows * 2 if wide else a.shape[0] // small_rows
        for a, wide in zip(key_arrays, wides)
    )
    total *= block_keys
    rows = parts * block_keys
    first = states is None
    if finish:
        each = [jax.ShapeDtypeStruct((rows + 16, width), bf16)]
    else:
        each = [
            jax.ShapeDtypeStruct((rows, 1), f32),
            jax.ShapeDtypeStruct((rows, 1), f32),
            jax.ShapeDtypeStruct((rows, width), f32),
        ]
    count = len(qs)
    given = gathered is not None
    args = [a for q in qs for a in q] + key_arrays + ([gathered] if given else []) + ([] if first else [a for state in states for a in state])
    out = pl.pallas_call(
        functools.partial(flash_kernel, wides, first, owns, finish, given),
        out_shape=each * count + ([jax.ShapeDtypeStruct((total, width), bf16)] if finish else []),
        in_specs=vmem_specs(len(args)),
        out_specs=vmem_specs(len(each) * count + finish),
        scratch_shapes=([] if finish or given else [pltpu.VMEM((total, width), bf16)])
        + [
            pltpu.VMEM((8, 128), bf16),
            pltpu.VMEM((count, rows, 1), f32),
        ],
        compiler_params=params,
        cost_estimate=pl.CostEstimate(
            flops=8 * count * rows * total * width,
            transcendentals=count * rows * total,
            bytes_accessed=2 * total * width + 6 * count * rows * width,
        ),
        name="flash",
    )(*args)
    if finish:
        return out
    return [tuple(out[3 * n : 3 * n + 3]) for n in range(count)]


def combine_kernel(m_ref, l_ref, acc_ref, other_ref, *out_refs):
    width = acc_ref.shape[1]
    rows = parts * block_keys
    tails = other_ref[rows : rows + 16, :].astype(f32)
    mixes, levels = [], []
    here = lax.broadcasted_iota(jnp.int32, (8, width), 0)
    for p in range(parts):
        at = slice(p * block_keys, (p + 1) * block_keys)
        level = column_of(
            tails[2 * p : 2 * p + 1, 0:256] + tails[2 * p + 1 : 2 * p + 2, 0:256]
        )
        peak = jnp.maximum(m_ref[at, :], level)
        mine = jnp.exp2(m_ref[at, :] - peak)
        theirs = jnp.exp2(level - peak)
        total = l_ref[at, :] * mine + theirs
        mixes.append(
            (acc_ref[at, :] * mine + other_ref[at, :].astype(f32) * theirs) / total
        )
        high, low = high_low((peak + jnp.log2(total)) * ln2)
        tail = jnp.where(here == p, row_of(high, width), 0.0) + jnp.where(
            here == 3 + p, row_of(low, width), 0.0
        )
        levels = tail if p == 0 else levels + tail
    for n in range(8):
        pieces = [
            mixes[p][n * filled + low - p * block_keys : n * filled + high - p * block_keys]
            for p in range(parts)
            for other, low, high in spans(p)
            if other == n
        ]
        out_refs[n][...] = jnp.concatenate(pieces + [levels], axis=0).astype(bf16)


def choose_kernel(me_ref, owner_ref, clusters_ref, rows_ref, lanes_ref, chosen_ref):
    _, packet, rank, part, lane = row_facts(
        clusters_ref[...].reshape(1, clusters_ref.shape[0]), owner_ref, me_ref[0]
    )
    count, total = rows_ref.shape
    target = column_of((packet * packet_rows + rank).astype(f32), count).astype(jnp.int32)
    at = lax.broadcasted_iota(jnp.int32, (count, total), 1)
    rows_ref[...] = (at == target).astype(f32).astype(bf16)
    lanes_ref[...] = ones_at(lanes_ref.shape[0], lane)
    chosen = hits(64, packet * 8 + part) | hits(64, packet * 8 + 3 + part)
    chosen_ref[...] = chosen.astype(f32)


def final_kernel(choice_ref, lanes_ref, chosen_ref, *refs):
    backs, (rows_ref, mass_ref, back) = refs[:8], refs[8:]
    for n in range(8):
        back[n * packet_rows : (n + 1) * packet_rows, :] = backs[n][...]
    rows_ref[...] = jnp.dot(
        choice_ref[...], back[...], preferred_element_type=f32
    ).astype(bf16)
    levels = jnp.concatenate(
        [backs[n][64:packet_rows, 0:256].astype(f32)[8:16] for n in range(8)], axis=0
    ).astype(bf16)
    found = jnp.dot(levels, lanes_ref[...], preferred_element_type=f32)
    mass_ref[...] = jnp.sum(
        jnp.where(chosen_ref[...] > 0.0, found, 0.0), axis=0, keepdims=True
    ).reshape(mass_ref.shape)


def links(mesh):
    side = 4

    def number(y, c, x, z):
        return ((y * 2 + c) * side + x) * side + z

    places = [
        (y, c, x, z) for y in range(side) for c in range(2) for x in range(side) for z in range(side)
    ]

    def pairs(move):
        return [(number(*at), number(*move(*at))) for at in places]

    dims = [
        pairs(lambda y, c, x, z: (y, c, x ^ 3, z)),
        pairs(lambda y, c, x, z: (y ^ 3, c, x, z)),
        pairs(lambda y, c, x, z: (y, c, x, z ^ 3)),
    ]
    swap = pairs(lambda y, c, x, z: (y, c ^ 1, x, z))
    trips = [
        pairs(lambda y, c, x, z, m=m: (y ^ (m >> 1 & 1), c, x ^ (m & 1), z ^ (m >> 2)))
        for m in (0, 1, 2, 4, 3, 5, 6, 7)
    ]
    return dims, swap, trips


def per_device(dims, swap, trips, embeddings, clusters, cluster_owner):
    rows, width = embeddings.shape
    send = lambda a, pairs: lax.ppermute(a, axes, pairs)
    group_axis, tile = lax.axis_index("group"), lax.axis_index("tile")
    kind = lambda at: (at + 1) // 2 % 2
    me = kind(tile // 4) + 2 * kind(group_axis // 2) + 4 * kind(tile % 4)
    me = me.astype(jnp.int32).reshape(1)
    smem = pl.BlockSpec(memory_space=pltpu.SMEM)
    packet = jax.ShapeDtypeStruct((packet_rows, width), bf16)
    packets = pl.pallas_call(
        place_kernel,
        out_shape=[packet] * 8,
        in_specs=[smem] + [pl.BlockSpec(memory_space=pltpu.HBM)] * 3,
        out_specs=vmem_specs(8),
        scratch_shapes=[
            pltpu.SMEM(cluster_owner.shape, jnp.int32),
            pltpu.VMEM(clusters.shape, jnp.int32),
            pltpu.VMEM(embeddings.shape, bf16),
            pltpu.SemaphoreType.DMA((3,)),
        ],
        compiler_params=params,
        name="place",
    )(
        me,
        *(pltpu.with_memory_space_constraint(a, pltpu.HBM) for a in (cluster_owner, clusters, embeddings)),
    )
    arrived = [packets[0]] + [send(packets[n], trips[n]) for n in range(1, 8)]
    big, small = pack((0, 1), arrived), pack((2,), arrived)
    wide = [
        [pair for pair in dims[s % 3] if pair[0] // 16 % 2 == 0]
        + [pair for pair in dims[(s + 1) % 3] if pair[0] // 16 % 2 == 1]
        for s in range(3)
    ]
    narrow = [dims[(s + 2) % 3] for s in range(3)]
    big0, small0 = send(big, wide[0]), send(small, narrow[0])
    q_own, q_other = (big, small), (send(big, swap), send(small, swap))
    big, small = jnp.concatenate([big, big0], axis=0), jnp.concatenate([small, small0], axis=0)
    big1, small1 = send(big, wide[1]), send(small, narrow[1])
    queries, owns = [q_other, q_own], [False, True]
    pairs = lambda *units: list(zip(units, (True, False) * 2))
    begin = pairs(*q_own, big0, small0)
    states = flash(queries[1:], owns[1:], begin, None, False)
    big, small, states[0] = lax.optimization_barrier((big, small, states[0]))
    states = flash(queries[:1], owns[:1], begin, None, False) + states
    big2, small2 = send(big, wide[2]), send(small, narrow[2])
    big3, small3 = send(big1, wide[2]), send(small1, narrow[2])
    states = flash(queries, owns, pairs(big1, small1), states, False)
    states = flash(queries, owns, pairs(big2, small2), states, False)
    partial, gathered = flash(queries[:1], owns[:1], pairs(big3, small3), states[:1], True)
    (mine,) = flash(queries[1:], owns[1:], pairs(big3, small3), states[1:], False, gathered)
    theirs = send(partial, swap)
    answers = pl.pallas_call(
        combine_kernel,
        out_shape=[packet] * 8,
        in_specs=vmem_specs(4),
        out_specs=vmem_specs(8),
        compiler_params=params,
        name="combine",
    )(*mine, theirs)
    back = [answers[0]] + [send(answers[n], trips[n]) for n in range(1, 8)]
    choice = pl.pallas_call(
        choose_kernel,
        out_shape=[
            jax.ShapeDtypeStruct((rows, 8 * packet_rows), bf16),
            jax.ShapeDtypeStruct((256, rows), bf16),
            jax.ShapeDtypeStruct((64, rows), f32),
        ],
        in_specs=[smem, smem] + vmem_specs(1),
        out_specs=vmem_specs(3),
        compiler_params=params,
        name="choose",
    )(me, cluster_owner, clusters)
    neighbours, log_mass = pl.pallas_call(
        final_kernel,
        out_shape=[jax.ShapeDtypeStruct((rows, width), bf16), jax.ShapeDtypeStruct((rows,), f32)],
        in_specs=vmem_specs(11),
        out_specs=vmem_specs(2),
        scratch_shapes=[pltpu.VMEM((8 * packet_rows, width), bf16)],
        compiler_params=params,
        name="final",
    )(*choice, *back)
    return neighbours, log_mass


def solution(mesh):
    placed = (P(axes, None), P(axes), P())
    dims, swap, trips = links(mesh)
    return jax.shard_map(
        functools.partial(per_device, dims, swap, trips),
        mesh=mesh,
        in_specs=placed,
        out_specs=(P(axes, None), P(axes)),
        check_vma=False,
    )
```
